512 devices in a mesh: replica: 4 (over z_hi, core), inner: 128 (over z_lo, x, y).
Axes of the slice: x: 4, y: 4, z: 16 (z_hi: 2, z_lo: 8; z = z_hi * 8 + z_lo), core: 2. Of those that a mesh axis runs over, the one named last changes fastest.
Arguments:
- square_weights: float32 [2, 1024, 1024], P(None, 'inner'), may hold values from -6 to 6
- square_copies: float32 [4, 2, 1024, 1024], P('replica', None, 'inner'), may hold values from -6 to 6
- square_moment: float32 [2, 1024, 1024], P(None, 'inner'), may hold values from -6 to 6
- broad_weights: float32 [2, 1024, 2048], P(None, 'inner'), may hold values from -6 to 6
- broad_copies: float32 [4, 2, 1024, 2048], P('replica', None, 'inner'), may hold values from -6 to 6
- broad_moment: float32 [2, 1024, 2048], P(None, 'inner'), may hold values from -6 to 6
- embed_weights: float32 [16384, 1024], P('inner'), may hold values from -6 to 6
- embed_copies: float32 [4, 16384, 1024], P('replica', 'inner'), may hold values from -90 to 90, as said below
- embed_moment: float32 [16384, 1024], P('inner'), may hold values from -6 to 6
- embed_error: float32 [4, 16384, 1024], P('replica', 'inner'), may hold values from -3 to 3
- warm_start: float32 [64, 1024], replicated, may hold values from -6 to 6
Outputs:
- square_updated: float32 [2, 1024, 1024], P(None, 'inner')
- square_velocity: float32 [2, 1024, 1024], P(None, 'inner')
- broad_updated: float32 [2, 1024, 2048], P(None, 'inner')
- broad_velocity: float32 [2, 1024, 2048], P(None, 'inner')
- embed_updated: float32 [16384, 1024], P('inner')
- embed_velocity: float32 [16384, 1024], P('inner')
- embed_carried: float32 [4, 16384, 1024], P('replica', 'inner')
The draws below stay inside these ranges and needn't reach their ends.
Inputs may be any that keep to these rules, and one draw needn't show every extreme that they name: `embed_copies`: each replica's embedding after its inner steps.
All inputs are finite; a program needn't handle non-finite values.
Results may differ from the reference program's by a relative error of at most 0.0001.
Values sent between devices are 32-bit elements; how exact they have to be, the bound alone decides.
A program may use at most 64 MiB of HBM per device.

```python
import math
import jax
import jax.numpy as jnp
from jax import lax

D = 1024
VDIM = 2048
VOCAB = 16384
RANK = 64
REPLICAS = 4


def embed_parts(key):
    base = jax.random.truncated_normal(jax.random.fold_in(key, 101), -6.0, 6.0, (VOCAB, D), jnp.float32)
    noise = jax.random.truncated_normal(jax.random.fold_in(key, 103), -6.0, 6.0, (REPLICAS, VOCAB, D), jnp.float32)
    rough = jax.random.uniform(jax.random.fold_in(key, 102), (VOCAB, 1), jnp.float32, 0.5, 1.0)
    ramp = jnp.arange(VOCAB, dtype=jnp.float32) / max(VOCAB - 1, 1)
    row_scale = 0.3 * jnp.exp(ramp * math.log(10.0))[:, None] * rough
    delta = row_scale * noise
    return (base, base[None] - delta)


def draw_embed_weights(key, part):
    return embed_parts(key)[0]


def draw_embed_copies(key, part):
    return embed_parts(key)[1]


def draw_warm_start(key, part):
    values = jax.random.truncated_normal(jax.random.fold_in(key, 201), -6.0, 6.0, (RANK, D), jnp.float32)
    spread = math.log(10.0)
    scales = jnp.exp(jax.random.uniform(jax.random.fold_in(key, 202), (RANK, 1), jnp.float32, 0.0, spread))
    return values * scales / 32.0


def block_scale(own_key, dims, split, smallest, top_value):
    def one(axis_at, parts):
        steps = jax.random.uniform(jax.random.fold_in(jax.random.fold_in(own_key, 6), axis_at), (parts,), jnp.float32, smallest / len(split), top_value / len(split))
        return jnp.repeat(jnp.exp(steps), dims[axis_at] // parts).reshape((-1,) + (1,) * (len(dims) - axis_at - 1))

    factor_of = one(*split[0])
    for cut in split[1:]:
        factor_of = factor_of * one(*cut)
    return factor_of


def centred(stream_key, shape, width, limit, pieces=(), held_as=jnp.bfloat16):
    entries = width * jax.random.normal(stream_key, shape, jnp.float32)
    if pieces:
        entries = entries * block_scale(stream_key, shape, pieces, -0.22, 0.18)
    return jnp.clip(entries, -limit, limit).astype(held_as)


def setup_inputs(seed: int = 0) -> dict:
    splits = jax.random.split(jax.random.key(seed), 12)
    square_weights = centred(splits[0], (2, D, D), 1.0, 6.0, ((1, 128),), jnp.float32)
    square_copies = centred(splits[1], (REPLICAS, 2, D, D), 1.0, 6.0, ((0, 4), (2, 128)), jnp.float32)
    square_moment = centred(splits[2], (2, D, D), 1.0, 6.0, ((1, 128),), jnp.float32)
    broad_weights = centred(splits[3], (2, D, VDIM), 1.0, 6.0, ((1, 128),), jnp.float32)
    broad_copies = centred(splits[4], (REPLICAS, 2, D, VDIM), 1.0, 6.0, ((0, 4), (2, 128)), jnp.float32)
    broad_moment = centred(splits[5], (2, D, VDIM), 1.0, 6.0, ((1, 128),), jnp.float32)
    embed_weights = draw_embed_weights(jax.random.fold_in(splits[11], 71), 0)
    embed_copies = draw_embed_copies(jax.random.fold_in(splits[11], 71), 0)
    embed_moment = centred(splits[8], (VOCAB, D), 1.0, 6.0, ((0, 128),), jnp.float32)
    embed_error = centred(splits[9], (REPLICAS, VOCAB, D), 0.5, 3.0, ((0, 4), (1, 128)), jnp.float32)
    warm_start = draw_warm_start(jax.random.fold_in(splits[11], 71), 0)
    return dict(square_weights=square_weights, square_copies=square_copies, square_moment=square_moment, broad_weights=broad_weights, broad_copies=broad_copies, broad_moment=broad_moment, embed_weights=embed_weights, embed_copies=embed_copies, embed_moment=embed_moment, embed_error=embed_error, warm_start=warm_start)


outer_rate = 0.7
momentum_decay = 0.9

def nesterov(weights, gradient, moment):
    velocity = momentum_decay * moment + gradient
    return (weights - outer_rate * (gradient + momentum_decay * velocity), velocity)

def reference(square_weights, square_copies, square_moment, broad_weights, broad_copies, broad_moment, embed_weights, embed_copies, embed_moment, embed_error, warm_start):
    highest = lax.Precision.HIGHEST
    contract_last = (((1,), (1,)), ((), ()))
    square_mean = jnp.sum(square_weights[None] - square_copies, axis=0) / REPLICAS
    broad_mean = jnp.sum(broad_weights[None] - broad_copies, axis=0) / REPLICAS
    square_updated, square_velocity = nesterov(square_weights, square_mean, square_moment)
    broad_updated, broad_velocity = nesterov(broad_weights, broad_mean, broad_moment)
    corrected = embed_weights[None] - embed_copies + embed_error
    left_factor = jnp.zeros((RANK, VOCAB), jnp.float32)
    for replica in range(REPLICAS):
        left_factor = left_factor + lax.dot_general(warm_start, corrected[replica], contract_last, precision=highest)
    left_factor = left_factor / REPLICAS
    gram_matrix = lax.dot_general(left_factor, left_factor, contract_last, precision=highest)
    lower_factor = jnp.linalg.cholesky(gram_matrix)
    basis_rows = lax.linalg.triangular_solve(lower_factor, left_factor, left_side=True, lower=True)
    right_factor = jnp.zeros((RANK, D), jnp.float32)
    for replica in range(REPLICAS):
        right_factor = right_factor + jnp.dot(basis_rows, corrected[replica], precision=highest)
    right_factor = right_factor / REPLICAS
    embed_step = lax.dot_general(basis_rows, right_factor, (((0,), (0,)), ((), ())), precision=highest)
    embed_carried = corrected - embed_step[None]
    embed_updated, embed_velocity = nesterov(embed_weights, embed_step, embed_moment)
    return (square_updated, square_velocity, broad_updated, broad_velocity, embed_updated, embed_velocity, embed_carried)
```

```python
import jax
import jax.numpy as jnp
from jax import lax
from jax.experimental import pallas as pl
from jax.experimental.pallas import tpu as pltpu
from jax.sharding import PartitionSpec as P

outer_rate = 0.7
momentum_decay = 0.9
MESH = pl.DeviceIdType.MESH
HIGHEST = lax.Precision.HIGHEST
PLANE = sorted(((dx, dy) for dx in range(4) for dy in range(4) if dx or dy), key=lambda d: -(min(d[0], 4 - d[0]) + min(d[1], 4 - d[1])))
RING = sorted(range(1, 16), key=lambda d: -min(d, 16 - d))


def dot(a, b):
    return jnp.dot(a, b, precision=HIGHEST, preferred_element_type=jnp.float32)


def dot_t(a, b):
    return lax.dot_general(a, b, (((1,), (1,)), ((), ())), precision=HIGHEST, preferred_element_type=jnp.float32)


def sub(v, j):
    return jnp.broadcast_to(v[j : j + 1, :], v.shape)


def lower_inverse(a):
    rows = lax.broadcasted_iota(jnp.int32, (8, 128), 0)
    scale = []
    for kb in range(8):
        cols = {}
        for j in range(8):
            lane = 64 + 8 * kb + j
            for b in range(kb, 8):
                cols[b, j] = jnp.broadcast_to(a[b][:, lane : lane + 1], (8, 128))
        inv_pivots = jnp.ones((8, 128), jnp.float32)
        for j in range(8):
            inv = 1.0 / sub(cols[kb, j], j)
            inv_pivots = jnp.where(rows == j, inv, inv_pivots)
            row = sub(a[kb], j)
            later = [sub(cols[kb, i], j) for i in range(j + 1, 8)]
            for b in range(kb, 8):
                factor = cols[b, j] * inv
                if b == kb:
                    factor = jnp.where(rows > j, factor, 0.0)
                a[b] = a[b] - factor * row
                for i in range(j + 1, 8):
                    cols[b, i] = cols[b, i] - factor * later[i - j - 1]
        scale.append(jnp.sqrt(inv_pivots))
    return [a[b] * scale[b] for b in range(8)]


def comm_kernel(
    sqw, sqc, brw, brc, ew, ec, ee, ws,
    sq_out, br_out, h_out, p_out,
    vsqw, vsqc, vbrw, vbrc, vew, vec, vee, vws,
    corr, corr_in, l_part, l_core, l_send, l_z, l_full, term, t_core, t_send, t_z, t_full,
    h_part, h_in, h_zs, h_z, h_full, g_part, g_in, g_zs, g_z, g_full,
    load_sem, one_send, one_recv, rs_send, rs_recv, grs_send, grs_recv, z_send, z_recv, gz_send, gz_recv,
    ag_send, ag_recv, gag_send, gag_recv, fw_send, fw_recv,
):
    rep, inn = lax.axis_index("replica"), lax.axis_index("inner")
    core, zhi = lax.rem(rep, 2), lax.div(rep, 2)
    zlo, x, y = lax.div(inn, 16), lax.rem(lax.div(inn, 4), 4), lax.rem(inn, 4)
    z, me = zhi * 8 + zlo, x * 4 + y
    other = 1 - core

    loads = []
    for i, (src, dst) in enumerate(((ew, vew), (ec, vec), (ee, vee), (ws, vws), (sqw, vsqw), (sqc, vsqc), (brw, vbrw), (brc, vbrc))):
        copy = pltpu.make_async_copy(src, dst, load_sem.at[i])
        copy.start()
        loads.append(copy)

    def plane(dx, dy):
        return lax.rem(x + dx, 4) * 4 + lax.rem(y + dy, 4)

    def at_z(d):
        return lax.rem(z + d, 16)

    def dev(c, zz, q):
        return (lax.div(zz, 8) * 2 + c, lax.rem(zz, 8) * 16 + q)

    partners = [dev(other, z, me)]
    for dx, dy in PLANE:
        partners += [dev(core, z, plane(dx, dy)), dev(other, z, plane(dx, dy))]
    for d in RING:
        partners.append(dev(core, at_z(d), me))
    barrier = pltpu.get_barrier_semaphore()
    for device in partners:
        pl.semaphore_signal(barrier, inc=1, device_id=device, device_id_type=MESH)

    sends = []

    def send(src, dst, ss, rs, device):
        copy = pltpu.make_async_remote_copy(src, dst, ss, rs, device_id=device, device_id_type=MESH)
        copy.start()
        sends.append(copy)
        return copy

    def arrived(dst, ss, rs):
        pltpu.make_async_remote_copy(dst, dst, ss, rs, device_id=partners[0], device_id_type=MESH).wait_recv()

    for i in range(4):
        loads[i].wait()
    corr[...] = vew[...] - vec[...] + vee[...]
    left = dot_t(vws[...], corr[...])
    l_part[0] = left[:32]
    l_part[1] = left[32:]
    pl.semaphore_wait(barrier, len(partners))
    twin = partners[0]
    send(l_part.at[other], l_core, one_send.at[0], one_recv.at[0], twin)
    send(corr, corr_in, one_send.at[1], one_recv.at[1], twin)
    for i in range(4, 8):
        loads[i].wait()
    for i in range(2):
        term[i] = vsqw[i] - vsqc[i]
        broad = vbrw[i] - vbrc[i]
        term[2 + 2 * i] = broad[:, :1024]
        term[3 + 2 * i] = broad[:, 1024:]
    send(term.at[pl.ds(3 * other, 3)], t_core, one_send.at[2], one_recv.at[2], twin)
    far = dev(core, at_z(8), me)
    arrived(l_core, one_send.at[0], one_recv.at[0])
    l_send[...] = l_part[core] + l_core[...]
    send(l_send, l_z, one_send.at[3], one_recv.at[3], far)
    arrived(t_core, one_send.at[2], one_recv.at[2])
    t_send[...] = term[pl.ds(3 * core, 3)] + t_core[...]
    send(t_send, t_z, one_send.at[4], one_recv.at[4], far)
    arrived(corr_in, one_send.at[1], one_recv.at[1])
    total = vew
    total[...] = corr[...] + corr_in[...]

    arrived(l_z, one_send.at[3], one_recv.at[3])
    mine = (l_send[...] + l_z[...]) * 0.25
    l_full[core] = mine
    send(l_full.at[core], l_full.at[core], one_send.at[5], one_recv.at[5], twin)
    for cb in range(4):
        block = dot(mine, total[:, 256 * cb : 256 * cb + 256]) * 0.25
        for rb in range(4):
            h_part[4 * rb + cb] = block[8 * rb : 8 * rb + 8]
    for i, (dx, dy) in enumerate(PLANE):
        q = plane(dx, dy)
        send(h_part.at[q], h_in.at[me], rs_send.at[i], rs_recv.at[me], dev(core, z, q))
    h_in[me] = h_part[me]

    arrived(l_full.at[other], one_send.at[5], one_recv.at[5])
    left_all = jnp.concatenate([l_full[0], l_full[1]], axis=0)
    nothing = jnp.zeros_like(left_all)
    packed = dot_t(mine[:16], jnp.concatenate([left_all, nothing], axis=0)) + dot_t(mine[16:], jnp.concatenate([nothing, left_all], axis=0))
    for i in range(16):
        g_part[i] = packed[i : i + 1]
    for i, (dx, dy) in enumerate(PLANE):
        q = plane(dx, dy)
        send(g_part.at[q], g_in.at[me], grs_send.at[i], grs_recv.at[me], dev(core, z, q))
    g_in[me] = g_part[me]

    def plane_wait(dst, ss, rs):
        for i, (dx, dy) in enumerate(PLANE):
            q = plane(dx, dy)
            arrived(dst.at[q], ss.at[i], rs.at[q])

    def added(ref, n):
        out = ref[0]
        for i in range(1, n):
            out = out + ref[i]
        return out

    plane_wait(g_in, grs_send, grs_recv)
    g_sum = added(g_in, 16)
    g_zs[...] = g_sum
    g_z[zlo] = g_sum
    for d in range(1, 8):
        peer = zhi * 8 + lax.rem(zlo + d, 8)
        send(g_zs, g_z.at[zlo], gz_send.at[d], gz_recv.at[zlo], dev(core, peer, me))
    plane_wait(h_in, rs_send, rs_recv)
    h_sum = added(h_in, 16)
    h_zs[...] = h_sum
    h_z[z] = h_sum
    for d in RING:
        send(h_zs, h_z.at[z], z_send.at[d], z_recv.at[z], dev(core, at_z(d), me))

    for d in range(1, 8):
        peer = lax.rem(zlo + d, 8)
        arrived(g_z.at[peer], gz_send.at[d], gz_recv.at[peer])
    g_full[core, me] = added(g_z, 8)
    mine_g = g_full.at[core, me]
    slot = core * 16 + me
    for i, (dx, dy) in enumerate(PLANE):
        q = plane(dx, dy)
        for k, c in enumerate((core, other)):
            send(mine_g, mine_g, gag_send.at[2 * i + k], gag_recv.at[slot], dev(c, z, q))
    send(mine_g, mine_g, gag_send.at[30], gag_recv.at[slot], twin)

    arrived(t_z, one_send.at[4], one_recv.at[4])
    t_full[pl.ds(3 * core, 3)] = (t_send[...] + t_z[...]) * 0.25
    send(t_full.at[pl.ds(3 * core, 3)], t_full.at[pl.ds(3 * core, 3)], one_send.at[6], one_recv.at[6], twin)

    for d in RING:
        peer = at_z(d)
        arrived(h_z.at[peer], z_send.at[d], z_recv.at[peer])
    h_full[core, me] = added(h_z, 16)
    mine_h = h_full.at[core, me]
    for i, (dx, dy) in enumerate(PLANE):
        send(mine_h, mine_h, ag_send.at[i], ag_recv.at[me], dev(core, z, plane(dx, dy)))
    send(mine_h, mine_h, fw_send.at[15], fw_recv.at[me], twin)

    for i, (dx, dy) in enumerate(PLANE):
        q = plane(dx, dy)
        for k, c in enumerate((core, other)):
            arrived(g_full.at[c, q], gag_send.at[2 * i + k], gag_recv.at[c * 16 + q])
    arrived(g_full.at[other, me], gag_send.at[30], gag_recv.at[other * 16 + me])

    lanes = lax.broadcasted_iota(jnp.int32, (8, 128), 1)
    rows = lax.broadcasted_iota(jnp.int32, (8, 128), 0)
    blocks = [None] * 8
    for c in range(2):
        for part in range(2):
            tile = jnp.concatenate([g_full[c, 8 * part + i] for i in range(8)], axis=0)
            blocks[4 * c + part] = pltpu.roll(tile, 64, 1)
            blocks[4 * c + 2 + part] = tile
    for b in range(8):
        blocks[b] = jnp.where(lanes >= 64, blocks[b], jnp.where(lanes == rows + 8 * b, 1.0, 0.0))
    inverse = jnp.concatenate(lower_inverse(blocks), axis=0)[:, :64]
    p_out[...] = dot(dot_t(left_all.T, inverse), inverse)

    for i, (dx, dy) in enumerate(PLANE):
        q = plane(dx, dy)
        arrived(h_full.at[core, q], ag_send.at[i], ag_recv.at[q])
        send(h_full.at[core, q], h_full.at[core, q], fw_send.at[i], fw_recv.at[q], twin)
    arrived(t_full.at[pl.ds(3 * other, 3)], one_send.at[6], one_recv.at[6])
    for i in range(2):
        sq_out[i] = t_full[i]
        br_out[i, :, :1024] = t_full[2 + 2 * i]
        br_out[i, :, 1024:] = t_full[3 + 2 * i]
    for i, (dx, dy) in enumerate(PLANE):
        q = plane(dx, dy)
        arrived(h_full.at[other, q], fw_send.at[i], fw_recv.at[q])
    arrived(h_full.at[other, me], fw_send.at[15], fw_recv.at[me])
    for c in range(2):
        for rb in range(4):
            for cb in range(4):
                h_out[32 * c + 8 * rb : 32 * c + 8 * rb + 8, 256 * cb : 256 * cb + 256] = h_full[c, 4 * rb + cb]
    for copy in sends:
        copy.wait_send()


def communicate(sqw, sqc, brw, brc, ew, ec, ee, ws):
    f32 = jnp.float32
    vmem = lambda *shape: pltpu.VMEM(shape, f32)
    dma = lambda n: pltpu.SemaphoreType.DMA((n,))
    return pl.pallas_call(
        comm_kernel,
        name="exchange",
        out_shape=(
            jax.ShapeDtypeStruct((2, 8, 1024), f32),
            jax.ShapeDtypeStruct((2, 8, 2048), f32),
            jax.ShapeDtypeStruct((64, 1024), f32),
            jax.ShapeDtypeStruct((128, 64), f32),
        ),
        in_specs=[pl.BlockSpec(memory_space=pl.ANY)] * 8,
        out_specs=tuple(pl.BlockSpec(memory_space=pltpu.VMEM) for _ in range(4)),
        scratch_shapes=[
            vmem(2, 8, 1024), vmem(2, 8, 1024), vmem(2, 8, 2048), vmem(2, 8, 2048),
            vmem(128, 1024), vmem(128, 1024), vmem(128, 1024), vmem(64, 1024),
            vmem(128, 1024), vmem(128, 1024), vmem(2, 32, 128), vmem(32, 128), vmem(32, 128), vmem(32, 128), vmem(2, 32, 128),
            vmem(6, 8, 1024), vmem(3, 8, 1024), vmem(3, 8, 1024), vmem(3, 8, 1024), vmem(6, 8, 1024),
            vmem(16, 8, 256), vmem(16, 8, 256), vmem(8, 256), vmem(16, 8, 256), vmem(2, 16, 8, 256),
            vmem(16, 1, 128), vmem(16, 1, 128), vmem(1, 128), vmem(8, 1, 128), vmem(2, 16, 1, 128),
            dma(8), dma(7), dma(7), dma(15), dma(16), dma(15), dma(16), dma(16), dma(16), dma(8), dma(8),
            dma(15), dma(16), dma(31), dma(32), dma(16), dma(16),
        ],
        compiler_params=pltpu.CompilerParams(collective_id=0, has_side_effects=True, vmem_limit_bytes=16 << 20),
    )(sqw, sqc, brw, brc, ew, ec, ee, ws)


def nesterov(weights, gradient, moment):
    velocity = momentum_decay * moment + gradient
    return (weights - outer_rate * (gradient + momentum_decay * velocity), velocity)


def update_kernel(sqs, sqw, sqm, brs, brw, brm, ew, ec, em, ee, p, h, squ, sqv, bru, brv, eu, ev, er):
    squ[...], sqv[...] = nesterov(sqw[...], sqs[...], sqm[...])
    bru[...], brv[...] = nesterov(brw[...], brs[...], brm[...])
    for cb in range(4):
        at = (slice(None), slice(256 * cb, 256 * cb + 256))
        step = dot(p[...], h[at])
        eu[at], ev[at] = nesterov(ew[at], step, em[at])
        er[at] = ew[at] - ec[at] + ee[at] - step


def local(
    square_weights,
    square_copies,
    square_moment,
    broad_weights,
    broad_copies,
    broad_moment,
    embed_weights,
    embed_copies,
    embed_moment,
    embed_error,
    warm_start,
):
    sq_sum, br_sum, h, p = communicate(
        square_weights, square_copies[0], broad_weights, broad_copies[0], embed_weights, embed_copies[0], embed_error[0], warm_start
    )
    shapes = [square_weights.shape] * 2 + [broad_weights.shape] * 2 + [embed_weights.shape] * 3
    outs = pl.pallas_call(
        update_kernel,
        name="update",
        out_shape=tuple(jax.ShapeDtypeStruct(s, jnp.float32) for s in shapes),
        compiler_params=pltpu.CompilerParams(vmem_limit_bytes=16 << 20),
    )(
        sq_sum, square_weights, square_moment, br_sum, broad_weights, broad_moment,
        embed_weights, embed_copies[0], embed_moment, embed_error[0], p, h,
    )
    return (*outs[:6], outs[6][None])


def solution(mesh):
    in_specs = (
        P(None, "inner", None),
        P("replica", None, "inner", None),
        P(None, "inner", None),
        P(None, "inner", None),
        P("replica", None, "inner", None),
        P(None, "inner", None),
        P("inner", None),
        P("replica", "inner", None),
        P("inner", None),
        P("replica", "inner", None),
        P(),
    )
    out_specs = (
        P(None, "inner", None),
        P(None, "inner", None),
        P(None, "inner", None),
        P(None, "inner", None),
        P("inner", None),
        P("inner", None),
        P("replica", "inner", None),
    )
    return jax.shard_map(local, mesh=mesh, in_specs=in_specs, out_specs=out_specs, check_vma=False)
```

```python
import jax
import jax.numpy as jnp
from jax import lax
from jax.experimental import pallas as pl
from jax.experimental.pallas import tpu as pltpu
from jax.sharding import PartitionSpec as P

outer_rate = 0.7
momentum_decay = 0.9
MESH = pl.DeviceIdType.MESH
HIGHEST = lax.Precision.HIGHEST
PLANE = sorted(((dx, dy) for dx in range(4) for dy in range(4) if dx or dy), key=lambda d: -(min(d[0], 4 - d[0]) + min(d[1], 4 - d[1])))
RING = sorted(range(1, 16), key=lambda d: -min(d, 16 - d))


def dot(a, b):
    return jnp.dot(a, b, precision=HIGHEST, preferred_element_type=jnp.float32)


def dot_t(a, b):
    return lax.dot_general(a, b, (((1,), (1,)), ((), ())), precision=HIGHEST, preferred_element_type=jnp.float32)


def sub(v, j):
    return jnp.broadcast_to(v[j : j + 1, :], v.shape)


def lower_inverse(a):
    rows = lax.broadcasted_iota(jnp.int32, (8, 128), 0)
    scale = []
    for kb in range(8):
        cols = {}
        for j in range(8):
            lane = 64 + 8 * kb + j
            for b in range(kb, 8):
                cols[b, j] = jnp.broadcast_to(a[b][:, lane : lane + 1], (8, 128))
        inv_pivots = jnp.ones((8, 128), jnp.float32)
        for j in range(8):
            inv = 1.0 / sub(cols[kb, j], j)
            inv_pivots = jnp.where(rows == j, inv, inv_pivots)
            row = sub(a[kb], j)
            later = [sub(cols[kb, i], j) for i in range(j + 1, 8)]
            for b in range(kb, 8):
                factor = cols[b, j] * inv
                if b == kb:
                    factor = jnp.where(rows > j, factor, 0.0)
                a[b] = a[b] - factor * row
                for i in range(j + 1, 8):
                    cols[b, i] = cols[b, i] - factor * later[i - j - 1]
        scale.append(jnp.sqrt(inv_pivots))
    return [a[b] * scale[b] for b in range(8)]


def comm_kernel(
    sqw, sqc, brw, brc, ew, ec, ee, ws, sqm, brm, em,
    o_squ, o_sqv, o_bru, o_brv, vew, vem, corr, p_out, h_out,
    vsqw, vsqc, vbrw, vbrc, vsqm, vbrm, vec, vee, vws,
    corr_in, l_part, l_in, l_full, term, t_core, t_send, t_z, t_full,
    h_part, h_in, h_zs, h_z, h_full, g_part, g_in, g_zs, g_z, g_full,
    load_sem, one_send, one_recv, rs_send, rs_recv, grs_send, grs_recv, z_send, z_recv, gz_send, gz_recv,
    ag_send, ag_recv, gag_send, gag_recv, fw_send, fw_recv,
):
    rep, inn = lax.axis_index("replica"), lax.axis_index("inner")
    core, zhi = lax.rem(rep, 2), lax.div(rep, 2)
    zlo, x, y = lax.div(inn, 16), lax.rem(lax.div(inn, 4), 4), lax.rem(inn, 4)
    z, me = zhi * 8 + zlo, x * 4 + y
    other = 1 - core

    def plane(dx, dy):
        return lax.rem(x + dx, 4) * 4 + lax.rem(y + dy, 4)

    def at_z(d):
        return lax.rem(z + d, 16)

    def dev(c, zz, q):
        return (lax.div(zz, 8) * 2 + c, lax.rem(zz, 8) * 16 + q)

    twin, far = dev(other, z, me), dev(core, at_z(8), me)
    partners = [dev(other, at_z(8), me)] + [dev(core, at_z(d), me) for d in RING]
    for dx, dy in PLANE:
        partners += [dev(core, z, plane(dx, dy)), dev(other, z, plane(dx, dy))]
    partners.append(twin)
    barrier = pltpu.get_barrier_semaphore()
    for device in partners:
        pl.semaphore_signal(barrier, inc=1, device_id=device, device_id_type=MESH)
    loads = []
    for i, (src, dst) in enumerate(((ew, vew), (ec, vec), (ee, vee), (ws, vws), (sqw, vsqw), (sqc, vsqc), (brw, vbrw), (brc, vbrc), (sqm, vsqm), (brm, vbrm), (em, vem))):
        copy = pltpu.make_async_copy(src, dst, load_sem.at[i])
        copy.start()
        loads.append(copy)

    sends = []

    def send(src, dst, ss, rs, device):
        copy = pltpu.make_async_remote_copy(src, dst, ss, rs, device_id=device, device_id_type=MESH)
        copy.start()
        sends.append(copy)
        return copy

    def arrived(dst, ss, rs):
        pltpu.make_async_remote_copy(dst, dst, ss, rs, device_id=twin, device_id_type=MESH).wait_recv()

    for i in range(4):
        loads[i].wait()
    corr[...] = vew[...] - vec[...] + vee[...]
    left = dot_t(vws[...], corr[...])
    l_part[0] = left[:32]
    l_part[1] = left[32:]
    pl.semaphore_wait(barrier, len(partners))
    peers = [(0, far), (1, dev(other, at_z(8), me)), (2, twin)]
    for i, device in peers:
        half = core if i == 0 else other
        send(l_part.at[half], l_in.at[rep], one_send.at[i], one_recv.at[rep], device)
    l_in[rep] = l_part[core]
    send(corr, corr_in, one_send.at[3], one_recv.at[4], twin)
    for i in range(4, 8):
        loads[i].wait()
    for i in range(2):
        term[i] = vsqw[i] - vsqc[i]
        broad = vbrw[i] - vbrc[i]
        term[2 + 2 * i] = broad[:, :1024]
        term[3 + 2 * i] = broad[:, 1024:]
    send(term.at[pl.ds(3 * other, 3)], t_core, one_send.at[4], one_recv.at[5], twin)
    arrived(t_core, one_send.at[4], one_recv.at[5])
    t_send[...] = term[pl.ds(3 * core, 3)] + t_core[...]
    send(t_send, t_z, one_send.at[5], one_recv.at[6], far)
    arrived(corr_in, one_send.at[3], one_recv.at[4])
    total = vec
    total[...] = corr[...] + corr_in[...]

    for k in range(1, 4):
        r = lax.rem(rep + k, 4)
        arrived(l_in.at[r], one_send.at[0], one_recv.at[r])
    mine = ((l_in[0] + l_in[1]) + (l_in[2] + l_in[3])) * 0.25
    l_full[core] = mine
    send(l_full.at[core], l_full.at[core], one_send.at[6], one_recv.at[7], twin)
    for cb in range(4):
        block = dot(mine, total[:, 256 * cb : 256 * cb + 256]) * 0.25
        for rb in range(4):
            h_part[4 * rb + cb] = block[8 * rb : 8 * rb + 8]
    for i, (dx, dy) in enumerate(PLANE):
        q = plane(dx, dy)
        send(h_part.at[q], h_in.at[me], rs_send.at[i], rs_recv.at[me], dev(core, z, q))
    h_in[me] = h_part[me]

    arrived(l_full.at[other], one_send.at[6], one_recv.at[7])
    left_all = jnp.concatenate([l_full[0], l_full[1]], axis=0)
    nothing = jnp.zeros_like(left_all)
    packed = dot_t(mine[:16], jnp.concatenate([left_all, nothing], axis=0)) + dot_t(mine[16:], jnp.concatenate([nothing, left_all], axis=0))
    for i in range(16):
        g_part[i] = packed[i : i + 1]
    for i, (dx, dy) in enumerate(PLANE):
        q = plane(dx, dy)
        send(g_part.at[q], g_in.at[me], grs_send.at[i], grs_recv.at[me], dev(core, z, q))
    g_in[me] = g_part[me]

    def plane_wait(dst, ss, rs):
        for i, (dx, dy) in enumerate(PLANE):
            q = plane(dx, dy)
            arrived(dst.at[q], ss.at[i], rs.at[q])

    def added(ref, n):
        out = ref[0]
        for i in range(1, n):
            out = out + ref[i]
        return out

    plane_wait(g_in, grs_send, grs_recv)
    g_sum = added(g_in, 16)
    g_zs[...] = g_sum
    g_z[zlo] = g_sum
    for d in range(1, 8):
        peer = zhi * 8 + lax.rem(zlo + d, 8)
        send(g_zs, g_z.at[zlo], gz_send.at[d], gz_recv.at[zlo], dev(core, peer, me))
    plane_wait(h_in, rs_send, rs_recv)
    h_sum = added(h_in, 16)
    h_zs[...] = h_sum
    h_z[z] = h_sum
    for d in RING:
        send(h_zs, h_z.at[z], z_send.at[d], z_recv.at[z], dev(core, at_z(d), me))

    for d in range(1, 8):
        peer = lax.rem(zlo + d, 8)
        arrived(g_z.at[peer], gz_send.at[d], gz_recv.at[peer])
    g_full[core, me] = added(g_z, 8)
    mine_g = g_full.at[core, me]
    slot = core * 16 + me
    for i, (dx, dy) in enumerate(PLANE):
        q = plane(dx, dy)
        for k, c in enumerate((core, other)):
            send(mine_g, mine_g, gag_send.at[2 * i + k], gag_recv.at[slot], dev(c, z, q))
    send(mine_g, mine_g, gag_send.at[30], gag_recv.at[slot], twin)

    arrived(t_z, one_send.at[5], one_recv.at[6])
    t_full[pl.ds(3 * core, 3)] = (t_send[...] + t_z[...]) * 0.25
    send(t_full.at[pl.ds(3 * core, 3)], t_full.at[pl.ds(3 * core, 3)], one_send.at[7], one_recv.at[8], twin)

    for d in RING:
        peer = at_z(d)
        arrived(h_z.at[peer], z_send.at[d], z_recv.at[peer])
    h_full[core, me] = added(h_z, 16)
    mine_h = h_full.at[core, me]
    for i, (dx, dy) in enumerate(PLANE):
        send(mine_h, mine_h, ag_send.at[i], ag_recv.at[me], dev(core, z, plane(dx, dy)))
    send(mine_h, mine_h, fw_send.at[15], fw_recv.at[me], twin)

    for i, (dx, dy) in enumerate(PLANE):
        q = plane(dx, dy)
        for k, c in enumerate((core, other)):
            arrived(g_full.at[c, q], gag_send.at[2 * i + k], gag_recv.at[c * 16 + q])
    arrived(g_full.at[other, me], gag_send.at[30], gag_recv.at[other * 16 + me])

    lanes = lax.broadcasted_iota(jnp.int32, (8, 128), 1)
    rows = lax.broadcasted_iota(jnp.int32, (8, 128), 0)
    blocks = [None] * 8
    for c in range(2):
        for part in range(2):
            tile = jnp.concatenate([g_full[c, 8 * part + i] for i in range(8)], axis=0)
            blocks[4 * c + part] = pltpu.roll(tile, 64, 1)
            blocks[4 * c + 2 + part] = tile
    for b in range(8):
        blocks[b] = jnp.where(lanes >= 64, blocks[b], jnp.where(lanes == rows + 8 * b, 1.0, 0.0))
    inverse = jnp.concatenate(lower_inverse(blocks), axis=0)[:, :64]
    p_out[...] = dot(dot_t(left_all.T, inverse), inverse)

    for i, (dx, dy) in enumerate(PLANE):
        q = plane(dx, dy)
        arrived(h_full.at[core, q], ag_send.at[i], ag_recv.at[q])
        send(h_full.at[core, q], h_full.at[core, q], fw_send.at[i], fw_recv.at[q], twin)
    arrived(t_full.at[pl.ds(3 * other, 3)], one_send.at[7], one_recv.at[8])
    for i in range(8, 11):
        loads[i].wait()
    for i in range(2):
        o_squ[i], o_sqv[i] = nesterov(vsqw[i], t_full[i], vsqm[i])
        for k in range(2):
            half = slice(1024 * k, 1024 * k + 1024)
            o_bru[i, :, half], o_brv[i, :, half] = nesterov(vbrw[i, :, half], t_full[2 + 2 * i + k], vbrm[i, :, half])
    for i, (dx, dy) in enumerate(PLANE):
        q = plane(dx, dy)
        arrived(h_full.at[other, q], fw_send.at[i], fw_recv.at[q])
    arrived(h_full.at[other, me], fw_send.at[15], fw_recv.at[me])
    h_out[...] = h_full[...]
    for copy in sends:
        copy.wait_send()


def communicate(*args):
    f32 = jnp.float32
    vmem = lambda *shape: pltpu.VMEM(shape, f32)
    dma = lambda n: pltpu.SemaphoreType.DMA((n,))
    shapes = [(2, 8, 1024)] * 2 + [(2, 8, 2048)] * 2 + [(128, 1024)] * 3 + [(128, 64), (2, 16, 8, 256)]
    return pl.pallas_call(
        comm_kernel,
        name="exchange",
        out_shape=tuple(jax.ShapeDtypeStruct(s, f32) for s in shapes),
        in_specs=[pl.BlockSpec(memory_space=pltpu.HBM)] * 11,
        out_specs=tuple(pl.BlockSpec(memory_space=pltpu.VMEM) for _ in shapes),
        scratch_shapes=[
            vmem(2, 8, 1024), vmem(2, 8, 1024), vmem(2, 8, 2048), vmem(2, 8, 2048), vmem(2, 8, 1024), vmem(2, 8, 2048),
            vmem(128, 1024), vmem(128, 1024), vmem(64, 1024),
            vmem(128, 1024), vmem(2, 32, 128), vmem(4, 32, 128), vmem(2, 32, 128),
            vmem(6, 8, 1024), vmem(3, 8, 1024), vmem(3, 8, 1024), vmem(3, 8, 1024), vmem(6, 8, 1024),
            vmem(16, 8, 256), vmem(16, 8, 256), vmem(8, 256), vmem(16, 8, 256), vmem(2, 16, 8, 256),
            vmem(16, 1, 128), vmem(16, 1, 128), vmem(1, 128), vmem(8, 1, 128), vmem(2, 16, 1, 128),
            dma(11), dma(8), dma(11), dma(15), dma(16), dma(15), dma(16), dma(16), dma(16), dma(8), dma(8),
            dma(15), dma(16), dma(31), dma(32), dma(16), dma(16),
        ],
        compiler_params=pltpu.CompilerParams(collective_id=0, has_side_effects=True, vmem_limit_bytes=16 << 20),
    )(*(pltpu.with_memory_space_constraint(v, pltpu.HBM) for v in args))


def nesterov(weights, gradient, moment):
    velocity = momentum_decay * moment + gradient
    return (weights - outer_rate * (gradient + momentum_decay * velocity), velocity)


def update_kernel(squ, sqv, bru, brv, ew, em, corr, p, h, o_squ, o_sqv, o_bru, o_brv, o_eu, o_ev, o_er, eu, ev, er, sems):
    copies = [pltpu.make_async_copy(src, dst, sems.at[i]) for i, (src, dst) in enumerate(((squ, o_squ), (sqv, o_sqv), (bru, o_bru), (brv, o_brv)))]
    for copy in copies:
        copy.start()
    for cb in range(4):
        at = (slice(None), slice(256 * cb, 256 * cb + 256))
        step = dot(p[...], jnp.concatenate([h[c, 4 * rb + cb] for c in range(2) for rb in range(4)], axis=0))
        eu[at], ev[at] = nesterov(ew[at], step, em[at])
        er[at] = corr[at] - step
        for i, (src, dst) in enumerate(((eu, o_eu), (ev, o_ev), (er, o_er))):
            copy = pltpu.make_async_copy(src.at[at], dst.at[at], sems.at[4 + 3 * cb + i])
            copy.start()
            copies.append(copy)
    for copy in copies:
        copy.wait()


def local(
    square_weights,
    square_copies,
    square_moment,
    broad_weights,
    broad_copies,
    broad_moment,
    embed_weights,
    embed_copies,
    embed_moment,
    embed_error,
    warm_start,
):
    ready = communicate(
        square_weights, square_copies[0], broad_weights, broad_copies[0], embed_weights, embed_copies[0], embed_error[0], warm_start,
        square_moment, broad_moment, embed_moment,
    )
    shapes = [square_weights.shape] * 2 + [broad_weights.shape] * 2 + [embed_weights.shape] * 3
    outs = pl.pallas_call(
        update_kernel,
        name="update",
        out_shape=tuple(jax.ShapeDtypeStruct(s, jnp.float32) for s in shapes),
        in_specs=[pl.BlockSpec(memory_space=pltpu.VMEM)] * 9,
        out_specs=tuple(pl.BlockSpec(memory_space=pltpu.HBM) for _ in shapes),
        scratch_shapes=[pltpu.VMEM((128, 1024), jnp.float32)] * 3 + [pltpu.SemaphoreType.DMA((16,))],
        compiler_params=pltpu.CompilerParams(vmem_limit_bytes=16 << 20),
    )(*ready)
    return (*outs[:6], outs[6][None])


def solution(mesh):
    in_specs = (
        P(None, "inner", None),
        P("replica", None, "inner", None),
        P(None, "inner", None),
        P(None, "inner", None),
        P("replica", None, "inner", None),
        P(None, "inner", None),
        P("inner", None),
        P("replica", "inner", None),
        P("inner", None),
        P("replica", "inner", None),
        P(),
    )
    out_specs = (
        P(None, "inner", None),
        P(None, "inner", None),
        P(None, "inner", None),
        P(None, "inner", None),
        P("inner", None),
        P("inner", None),
        P("replica", "inner", None),
    )
    return jax.shard_map(local, mesh=mesh, in_specs=in_specs, out_specs=out_specs, check_vma=False)
```

```python
import jax
import jax.numpy as jnp
from jax import lax
from jax.experimental import pallas as pl
from jax.experimental.pallas import tpu as pltpu
from jax.sharding import PartitionSpec as P

outer_rate = 0.7
momentum_decay = 0.9
MESH = pl.DeviceIdType.MESH
HIGHEST = lax.Precision.HIGHEST


def hops(dx, dy):
    return min(dx, 4 - dx) + min(dy, 4 - dy)


PLANE = sorted(((dx, dy) for dx in range(4) for dy in range(4) if dx or dy), key=lambda d: -hops(*d))
FAR = sum(hops(*d) > 0 for d in PLANE)
RING = sorted(range(1, 16), key=lambda d: -min(d, 16 - d))


def dot(a, b):
    return jnp.dot(a, b, precision=HIGHEST, preferred_element_type=jnp.float32)


def dot_t(a, b):
    return lax.dot_general(a, b, (((1,), (1,)), ((), ())), precision=HIGHEST, preferred_element_type=jnp.float32)


def sub(v, j):
    return jnp.broadcast_to(v[j : j + 1, :], v.shape)


def lower_inverse(a):
    rows = lax.broadcasted_iota(jnp.int32, (8, 128), 0)
    scale = []
    for kb in range(8):
        cols = {}
        for j in range(8):
            lane = 64 + 8 * kb + j
            for b in range(kb, 8):
                cols[b, j] = jnp.broadcast_to(a[b][:, lane : lane + 1], (8, 128))
        inv_pivots = jnp.ones((8, 128), jnp.float32)
        for j in range(8):
            inv = 1.0 / sub(cols[kb, j], j)
            inv_pivots = jnp.where(rows == j, inv, inv_pivots)
            row = sub(a[kb], j)
            later = [sub(cols[kb, i], j) for i in range(j + 1, 8)]
            for b in range(kb, 8):
                factor = cols[b, j] * inv
                if b == kb:
                    factor = jnp.where(rows > j, factor, 0.0)
                a[b] = a[b] - factor * row
                for i in range(j + 1, 8):
                    cols[b, i] = cols[b, i] - factor * later[i - j - 1]
        scale.append(jnp.sqrt(inv_pivots))
    return [a[b] * scale[b] for b in range(8)]


def comm_kernel(
    sqw, sqc, brw, brc, ew, ec, ee, ws, sqm, brm, em,
    o_squ, o_sqv, o_bru, o_brv, vew, vem, corr, p_out, h_out,
    vsqw, vsqc, vbrw, vbrc, vsqm, vbrm, vec, vee, vws,
    corr_in, l_part, l_twin, l_chip, l_in, l_relay, l_full, g_side, term, t_core, t_send, t_relay, t_z, t_full,
    h_part, h_in, h_zs, h_z, h_full, g_part, g_in, g_zs, g_z, g_full,
    load_sem, sent, got, piece_sem,
):
    rep, inn = lax.axis_index("replica"), lax.axis_index("inner")
    core, zhi = lax.rem(rep, 2), lax.div(rep, 2)
    zlo, x, y = lax.div(inn, 16), lax.rem(lax.div(inn, 4), 4), lax.rem(inn, 4)
    z, me = zhi * 8 + zlo, x * 4 + y
    other = 1 - core

    def plane(dx, dy):
        return lax.rem(x + dx, 4) * 4 + lax.rem(y + dy, 4)

    def at_z(d):
        return lax.rem(z + d, 16)

    def dev(c, zz, q):
        return (lax.div(zz, 8) * 2 + c, lax.rem(zz, 8) * 16 + q)

    twin, ahead, behind = dev(other, z, me), at_z(4), at_z(12)
    partners = [dev(other, ahead, me), dev(other, behind, me)] + [dev(core, at_z(d), me) for d in (4, 12, 3, 13, 2, 14, 1, 15)]
    for dx, dy in PLANE:
        partners += [dev(core, z, plane(dx, dy)), dev(other, z, plane(dx, dy))]
    partners.append(twin)
    barrier = pltpu.get_barrier_semaphore()
    for device in partners:
        pl.semaphore_signal(barrier, inc=1, device_id=device, device_id_type=MESH)
    loads = []
    for i, (src, dst) in enumerate(((ew, vew), (ec, vec), (ee, vee), (ws, vws), (sqw, vsqw), (sqc, vsqc), (brw, vbrw), (brc, vbrc), (sqm, vsqm), (brm, vbrm), (em, vem))):
        copy = pltpu.make_async_copy(src, dst, load_sem.at[i])
        copy.start()
        loads.append(copy)

    def send(src, dst, stage, device, arrival=None):
        pltpu.make_async_remote_copy(src, dst, sent.at[stage], got.at[stage] if arrival is None else arrival, device_id=device, device_id_type=MESH).start()

    def copies(ref, stage, arrival=None):
        return pltpu.make_async_remote_copy(ref, ref, sent.at[stage], got.at[stage] if arrival is None else arrival, device_id=twin, device_id_type=MESH)

    def arrived(ref, stage):
        copies(ref, stage).wait_recv()

    def left(ref, stage):
        copies(ref, stage).wait_send()

    def first(ref, n):
        return ref.at[pl.ds(0, n)]

    def added(ref, n):
        out = ref[0]
        for i in range(1, n):
            out = out + ref[i]
        return out

    for i in range(4):
        loads[i].wait()
    corr[...] = vew[...] - vec[...] + vee[...]
    part = dot_t(vws[...], corr[...])
    l_part[0] = part[:32]
    l_part[1] = part[32:]
    pl.semaphore_wait(barrier, len(partners))
    send(l_part.at[0], l_relay.at[0], 13, dev(core, ahead, me))
    send(l_part.at[1], l_relay.at[1], 14, dev(core, behind, me))
    send(l_part, l_twin, 17, twin)
    for i in range(4, 8):
        loads[i].wait()
    for i in range(2):
        for k in range(2):
            half = slice(512 * k, 512 * k + 512)
            term[2 * i + k] = vsqw[i, :, half] - vsqc[i, :, half]
        for k in range(4):
            half = slice(512 * k, 512 * k + 512)
            term[4 + 4 * i + k] = vbrw[i, :, half] - vbrc[i, :, half]
    mine_t, other_t = pl.ds(6 * core, 6), pl.ds(6 * other, 6)
    send(term.at[other_t], t_core, 1, twin)
    send(corr, corr_in, 2, twin)
    arrived(t_core, 1)
    t_send[...] = term[mine_t] + t_core[...]
    low, high = pl.ds(0, 3), pl.ds(3, 3)
    send(t_send.at[low], t_relay.at[0], 15, dev(core, ahead, me))
    send(t_send.at[high], t_relay.at[1], 16, dev(core, behind, me))
    arrived(l_relay.at[0], 13)
    send(l_relay.at[0], l_in.at[core], 0, dev(0, ahead, me))
    arrived(l_relay.at[1], 14)
    send(l_relay.at[1], l_in.at[core], 0, dev(1, behind, me))
    arrived(corr_in, 2)
    total = vec
    total[...] = corr[...] + corr_in[...]
    left(t_core, 1)
    left(corr, 2)
    arrived(l_twin, 17)
    left(l_part, 17)
    l_chip[...] = l_part[...] + l_twin[...]
    chip = jnp.concatenate([l_chip[0], l_chip[1]], axis=0) * 0.25
    nothing = jnp.zeros_like(chip)
    g_side[0] = jnp.concatenate([chip, nothing], axis=0)
    g_side[1] = jnp.concatenate([nothing, chip], axis=0)
    left(l_part.at[0], 13)
    left(l_part.at[1], 14)
    arrived(t_relay.at[0], 15)
    send(t_relay.at[0], t_z.at[low], 3, dev(core, ahead, me))
    arrived(t_relay.at[1], 16)
    send(t_relay.at[1], t_z.at[high], 3, dev(core, behind, me))
    left(t_send.at[low], 15)
    left(t_send.at[high], 16)

    arrived(l_in, 0)
    mine = (l_chip[core] + (l_in[0] + l_in[1])) * 0.25
    for cb in range(4):
        block = dot(mine, total[:, 256 * cb : 256 * cb + 256]) * 0.25
        for rb in range(4):
            h_part[4 * rb + cb] = block[8 * rb : 8 * rb + 8]
    for dx, dy in PLANE:
        q = plane(dx, dy)
        send(h_part.at[q], h_in.at[me], 5, dev(core, z, q))
    h_in[me] = h_part[me]

    packed = dot_t(mine[:16], g_side[0]) + dot_t(mine[16:], g_side[1])
    for i in range(16):
        g_part[i] = packed[i : i + 1]
    for dx, dy in PLANE:
        q = plane(dx, dy)
        send(g_part.at[q], g_in.at[me], 6, dev(core, z, q))
    g_in[me] = g_part[me]
    l_full[core] = mine
    send(l_full.at[core], l_full.at[core], 4, twin)
    left(l_in, 0)

    arrived(first(g_in, 15), 6)
    g_sum = added(g_in, 16)
    g_zs[...] = g_sum
    g_z[z] = g_sum
    for d in RING:
        send(g_zs, g_z.at[z], 8, dev(core, at_z(d), me))
    arrived(first(h_in, 15), 5)
    h_sum = added(h_in, 16)
    h_zs[...] = h_sum
    h_z[z] = h_sum
    for d in RING:
        send(h_zs, h_z.at[z], 7, dev(core, at_z(d), me))
    left(first(h_in, 15), 5)
    left(first(g_in, 15), 6)

    arrived(t_z, 3)
    t_full[mine_t] = (t_send[...] + t_z[...]) * 0.25
    send(t_full.at[mine_t], t_full.at[mine_t], 9, twin)
    left(t_send, 3)
    for i in range(8, 11):
        loads[i].wait()

    arrived(l_full.at[other], 4)
    left(l_full.at[core], 4)
    arrived(first(g_z, 15), 8)
    slot = core * 16 + me
    g_full[slot] = added(g_z, 16)
    for dx, dy in PLANE:
        for c in (core, other):
            send(g_full.at[slot], g_full.at[slot], 10, dev(c, z, plane(dx, dy)))
    send(g_full.at[slot], g_full.at[slot], 10, twin)
    left(first(g_z, 15), 8)

    arrived(first(h_z, 15), 7)
    h_full[slot] = added(h_z, 16)
    for dx, dy in PLANE:
        send(h_full.at[slot], h_full.at[slot], 11, dev(core, z, plane(dx, dy)), piece_sem.at[me])
        if hops(dx, dy) > 0:
            send(h_full.at[slot], h_full.at[slot], 11, dev(other, z, plane(dx, dy)), got.at[12])
    send(h_full.at[slot], h_full.at[slot], 12, twin)
    left(first(h_z, 15), 7)

    arrived(t_full.at[other_t], 9)
    left(t_full.at[mine_t], 9)
    for i in range(2):
        for k in range(2):
            half = slice(512 * k, 512 * k + 512)
            o_squ[i, :, half], o_sqv[i, :, half] = nesterov(vsqw[i, :, half], t_full[2 * i + k], vsqm[i, :, half])
        for k in range(4):
            half = slice(512 * k, 512 * k + 512)
            o_bru[i, :, half], o_brv[i, :, half] = nesterov(vbrw[i, :, half], t_full[4 + 4 * i + k], vbrm[i, :, half])

    arrived(first(g_full, 31), 10)
    lanes = lax.broadcasted_iota(jnp.int32, (8, 128), 1)
    rows = lax.broadcasted_iota(jnp.int32, (8, 128), 0)
    blocks = [None] * 8
    for c in range(2):
        for half in range(2):
            tile = jnp.concatenate([g_full[16 * c + 8 * half + i] for i in range(8)], axis=0)
            blocks[4 * c + half] = pltpu.roll(tile, 64, 1)
            blocks[4 * c + 2 + half] = tile
    for b in range(8):
        blocks[b] = jnp.where(lanes >= 64, blocks[b], jnp.where(lanes == rows + 8 * b, 1.0, 0.0))
    inverse = jnp.concatenate(lower_inverse(blocks), axis=0)[:, :64]
    p_out[...] = dot(dot_t(jnp.concatenate([l_full[0], l_full[1]], axis=0).T, inverse), inverse)
    left(first(g_full, 31), 10)

    for dx, dy in reversed(PLANE):
        q = plane(dx, dy)
        at = core * 16 + q
        copies(h_full.at[at], 11, piece_sem.at[q]).wait_recv()
        if hops(dx, dy) <= 0:
            send(h_full.at[at], h_full.at[at], 12, twin)
    left(first(h_full, 15 + FAR), 11)
    arrived(first(h_full, 16), 12)
    h_out[...] = h_full[...]
    left(first(h_full, 16 - FAR), 12)


def communicate(*args):
    f32 = jnp.float32
    vmem = lambda *shape: pltpu.VMEM(shape, f32)
    dma = lambda n: pltpu.SemaphoreType.DMA((n,))
    shapes = [(2, 8, 1024)] * 2 + [(2, 8, 2048)] * 2 + [(128, 1024)] * 3 + [(128, 64), (32, 8, 256)]
    return pl.pallas_call(
        comm_kernel,
        name="exchange",
        out_shape=tuple(jax.ShapeDtypeStruct(s, f32) for s in shapes),
        in_specs=[pl.BlockSpec(memory_space=pltpu.HBM)] * 11,
        out_specs=tuple(pl.BlockSpec(memory_space=pltpu.VMEM) for _ in shapes),
        scratch_shapes=[
            vmem(2, 8, 1024), vmem(2, 8, 1024), vmem(2, 8, 2048), vmem(2, 8, 2048), vmem(2, 8, 1024), vmem(2, 8, 2048),
            vmem(128, 1024), vmem(128, 1024), vmem(64, 1024),
            vmem(128, 1024), vmem(2, 32, 128), vmem(2, 32, 128), vmem(2, 32, 128), vmem(2, 32, 128), vmem(2, 32, 128), vmem(2, 32, 128), vmem(2, 128, 128),
            vmem(12, 8, 512), vmem(6, 8, 512), vmem(6, 8, 512), vmem(2, 3, 8, 512), vmem(6, 8, 512), vmem(12, 8, 512),
            vmem(16, 8, 256), vmem(16, 8, 256), vmem(8, 256), vmem(16, 8, 256), vmem(32, 8, 256),
            vmem(16, 1, 128), vmem(16, 1, 128), vmem(1, 128), vmem(16, 1, 128), vmem(32, 1, 128),
            dma(11), dma(18), dma(18), dma(16),
        ],
        compiler_params=pltpu.CompilerParams(collective_id=0, has_side_effects=True, vmem_limit_bytes=16 << 20),
    )(*(pltpu.with_memory_space_constraint(v, pltpu.HBM) for v in args))


def nesterov(weights, gradient, moment):
    velocity = momentum_decay * moment + gradient
    return (weights - outer_rate * (gradient + momentum_decay * velocity), velocity)


def update_kernel(squ, sqv, bru, brv, ew, em, corr, p, h, o_squ, o_sqv, o_bru, o_brv, o_eu, o_ev, o_er, eu, ev, er, sems):
    copies = [pltpu.make_async_copy(src, dst, sems.at[i]) for i, (src, dst) in enumerate(((squ, o_squ), (sqv, o_sqv), (bru, o_bru), (brv, o_brv)))]
    for copy in copies:
        copy.start()
    for cb in range(4):
        at = (slice(None), slice(256 * cb, 256 * cb + 256))
        step = dot(p[...], jnp.concatenate([h[16 * c + 4 * rb + cb] for c in range(2) for rb in range(4)], axis=0))
        eu[at], ev[at] = nesterov(ew[at], step, em[at])
        er[at] = corr[at] - step
        for i, (src, dst) in enumerate(((eu, o_eu), (ev, o_ev), (er, o_er))):
            copy = pltpu.make_async_copy(src.at[at], dst.at[at], sems.at[4 + 3 * cb + i])
            copy.start()
            copies.append(copy)
    for copy in copies:
        copy.wait()


def local(
    square_weights,
    square_copies,
    square_moment,
    broad_weights,
    broad_copies,
    broad_moment,
    embed_weights,
    embed_copies,
    embed_moment,
    embed_error,
    warm_start,
):
    ready = communicate(
        square_weights, square_copies[0], broad_weights, broad_copies[0], embed_weights, embed_copies[0], embed_error[0], warm_start,
        square_moment, broad_moment, embed_moment,
    )
    shapes = [square_weights.shape] * 2 + [broad_weights.shape] * 2 + [embed_weights.shape] * 3
    outs = pl.pallas_call(
        update_kernel,
        name="update",
        out_shape=tuple(jax.ShapeDtypeStruct(s, jnp.float32) for s in shapes),
        in_specs=[pl.BlockSpec(memory_space=pltpu.VMEM)] * 9,
        out_specs=tuple(pl.BlockSpec(memory_space=pltpu.HBM) for _ in shapes),
        scratch_shapes=[pltpu.VMEM((128, 1024), jnp.float32)] * 3 + [pltpu.SemaphoreType.DMA((16,))],
        compiler_params=pltpu.CompilerParams(vmem_limit_bytes=16 << 20),
    )(*ready)
    return (*outs[:6], outs[6][None])


def solution(mesh):
    in_specs = (
        P(None, "inner", None),
        P("replica", None, "inner", None),
        P(None, "inner", None),
        P(None, "inner", None),
        P("replica", None, "inner", None),
        P(None, "inner", None),
        P("inner", None),
        P("replica", "inner", None),
        P("inner", None),
        P("replica", "inner", None),
        P(),
    )
    out_specs = (
        P(None, "inner", None),
        P(None, "inner", None),
        P(None, "inner", None),
        P(None, "inner", None),
        P("inner", None),
        P("inner", None),
        P("replica", "inner", None),
    )
    return jax.shard_map(local, mesh=mesh, in_specs=in_specs, out_specs=out_specs, check_vma=False)
```

```python
import jax
import jax.numpy as jnp
from jax import lax
from jax.experimental import pallas as pl
from jax.experimental.pallas import tpu as pltpu
from jax.sharding import PartitionSpec as P

outer_rate = 0.7
momentum_decay = 0.9
MESH = pl.DeviceIdType.MESH
HIGHEST = lax.Precision.HIGHEST


def hops(dx, dy):
    return min(dx, 4 - dx) + min(dy, 4 - dy)


PLANE = sorted(((dx, dy) for dx in range(4) for dy in range(4) if dx or dy), key=lambda d: -hops(*d))
RING = sorted(range(1, 16), key=lambda d: -min(d, 16 - d))


def dot(a, b):
    return jnp.dot(a, b, precision=HIGHEST, preferred_element_type=jnp.float32)


def dot_t(a, b):
    return lax.dot_general(a, b, (((1,), (1,)), ((), ())), precision=HIGHEST, preferred_element_type=jnp.float32)


def sub(v, j):
    return jnp.broadcast_to(v[j : j + 1, :], v.shape)


def lower_inverse(a):
    rows = lax.broadcasted_iota(jnp.int32, (8, 128), 0)
    scale = []
    for kb in range(8):
        cols = {}
        for j in range(8):
            lane = 64 + 8 * kb + j
            for b in range(kb, 8):
                cols[b, j] = jnp.broadcast_to(a[b][:, lane : lane + 1], (8, 128))
        inv_pivots = jnp.ones((8, 128), jnp.float32)
        for j in range(8):
            inv = 1.0 / sub(cols[kb, j], j)
            inv_pivots = jnp.where(rows == j, inv, inv_pivots)
            row = sub(a[kb], j)
            later = [sub(cols[kb, i], j) for i in range(j + 1, 8)]
            for b in range(kb, 8):
                factor = cols[b, j] * inv
                if b == kb:
                    factor = jnp.where(rows > j, factor, 0.0)
                a[b] = a[b] - factor * row
                for i in range(j + 1, 8):
                    cols[b, i] = cols[b, i] - factor * later[i - j - 1]
        scale.append(jnp.sqrt(inv_pivots))
    return [a[b] * scale[b] for b in range(8)]


def comm_kernel(
    sqw, sqc, brw, brc, ew, ec, ee, ws, sqm, brm, em,
    o_squ, o_sqv, o_bru, o_brv, vew, vem, corr, p_out, h_out,
    vsqw, vsqc, vbrw, vbrc, vsqm, vbrm, vec, vee, vws,
    corr_in, l_part, l_twin, l_chip, l_in, l_relay, l_full, g_side, term, t_core, t_send, t_relay, t_z, t_full,
    h_part, h_in, h_zs, h_z, h_full, g_part, g_in, g_zs, g_z, g_full,
    load_sem, sent, got,
):
    rep, inn = lax.axis_index("replica"), lax.axis_index("inner")
    core, zhi = lax.rem(rep, 2), lax.div(rep, 2)
    zlo, x, y = lax.div(inn, 16), lax.rem(lax.div(inn, 4), 4), lax.rem(inn, 4)
    z, me = zhi * 8 + zlo, x * 4 + y
    other = 1 - core

    def plane(dx, dy):
        return lax.rem(x + dx, 4) * 4 + lax.rem(y + dy, 4)

    def at_z(d):
        return lax.rem(z + d, 16)

    def dev(c, zz, q):
        return (lax.div(zz, 8) * 2 + c, lax.rem(zz, 8) * 16 + q)

    twin, ahead, behind = dev(other, z, me), at_z(4), at_z(12)
    partners = [dev(other, ahead, me), dev(other, behind, me)] + [dev(core, at_z(d), me) for d in (4, 12, 3, 13, 2, 14, 1, 15)]
    for dx, dy in PLANE:
        partners += [dev(core, z, plane(dx, dy)), dev(other, z, plane(dx, dy))]
    partners.append(twin)
    loads = [
        pltpu.make_async_copy(src, dst, load_sem.at[i])
        for i, (src, dst) in enumerate((
            (ew, vew), (ec, vec), (ee, vee), (ws, vws), (sqw, vsqw), (sqc, vsqc), (brw, vbrw), (brc, vbrc), (sqm, vsqm), (brm, vbrm), (em, vem)
        ))
    ]
    for i in range(4):
        loads[i].start()
    barrier = pltpu.get_barrier_semaphore()
    for device in partners:
        pl.semaphore_signal(barrier, inc=1, device_id=device, device_id_type=MESH)
    for i in range(4, 11):
        loads[i].start()

    def send(src, dst, stage, device, arrival=None):
        pltpu.make_async_remote_copy(src, dst, sent.at[stage], got.at[stage] if arrival is None else arrival, device_id=device, device_id_type=MESH).start()

    def copies(ref, stage, arrival=None):
        return pltpu.make_async_remote_copy(ref, ref, sent.at[stage], got.at[stage] if arrival is None else arrival, device_id=twin, device_id_type=MESH)

    def arrived(ref, stage):
        copies(ref, stage).wait_recv()

    def left(ref, stage):
        copies(ref, stage).wait_send()

    def first(ref, n):
        return ref.at[pl.ds(0, n)]

    def added(ref, n):
        out = ref[0]
        for i in range(1, n):
            out = out + ref[i]
        return out

    for i in range(4):
        loads[i].wait()
    corr[...] = vew[...] - vec[...] + vee[...]
    part = dot_t(vws[...], corr[...])
    l_part[0] = part[:32]
    l_part[1] = part[32:]
    pl.semaphore_wait(barrier, len(partners))

    send(l_part.at[0], l_relay.at[0], 13, dev(core, ahead, me))
    send(l_part.at[1], l_relay.at[1], 14, dev(core, behind, me))
    send(l_part, l_twin, 17, twin)
    for i in range(4, 8):
        loads[i].wait()
    for i in range(2):
        for k in range(2):
            half = slice(512 * k, 512 * k + 512)
            term[2 * i + k] = vsqw[i, :, half] - vsqc[i, :, half]
        for k in range(4):
            half = slice(512 * k, 512 * k + 512)
            term[4 + 4 * i + k] = vbrw[i, :, half] - vbrc[i, :, half]
    mine_t, other_t = pl.ds(6 * core, 6), pl.ds(6 * other, 6)
    send(term.at[other_t], t_core, 1, twin)
    send(corr, corr_in, 2, twin)
    arrived(t_core, 1)
    t_send[...] = term[mine_t] + t_core[...]
    low, high = pl.ds(0, 3), pl.ds(3, 3)
    send(t_send.at[low], t_relay.at[0], 15, dev(core, ahead, me))
    send(t_send.at[high], t_relay.at[1], 16, dev(core, behind, me))
    arrived(l_relay.at[0], 13)
    send(l_relay.at[0], l_in.at[core], 0, dev(0, ahead, me))
    arrived(l_relay.at[1], 14)
    send(l_relay.at[1], l_in.at[core], 0, dev(1, behind, me))
    arrived(corr_in, 2)
    total = vec
    total[...] = corr[...] + corr_in[...]
    left(t_core, 1)
    left(corr, 2)
    arrived(l_twin, 17)
    left(l_part, 17)
    l_chip[...] = l_part[...] + l_twin[...]
    chip = jnp.concatenate([l_chip[0], l_chip[1]], axis=0) * 0.25
    nothing = jnp.zeros_like(chip)
    g_side[0] = jnp.concatenate([chip, nothing], axis=0)
    g_side[1] = jnp.concatenate([nothing, chip], axis=0)

    left(l_part.at[0], 13)
    left(l_part.at[1], 14)
    arrived(l_in, 0)
    mine = (l_chip[core] + (l_in[0] + l_in[1])) * 0.25
    packed = dot_t(mine[:16], g_side[0]) + dot_t(mine[16:], g_side[1])
    for i in range(16):
        g_part[i] = packed[i : i + 1]
    for dx, dy in PLANE:
        q = plane(dx, dy)
        send(g_part.at[q], g_in.at[me], 6, dev(core, z, q))
    for cb in range(4):
        block = dot(mine, total[:, 256 * cb : 256 * cb + 256]) * 0.25
        for rb in range(4):
            h_part[4 * rb + cb] = block[8 * rb : 8 * rb + 8]
    for dx, dy in PLANE:
        q = plane(dx, dy)
        send(h_part.at[q], h_in.at[me], 5, dev(core, z, q))
    g_in[me] = g_part[me]
    h_in[me] = h_part[me]
    l_full[core] = mine
    send(l_full.at[core], l_full.at[core], 4, twin)
    left(l_in, 0)
    arrived(t_relay.at[0], 15)
    send(t_relay.at[0], t_z.at[low], 3, dev(core, ahead, me))
    arrived(t_relay.at[1], 16)
    send(t_relay.at[1], t_z.at[high], 3, dev(core, behind, me))
    left(t_send.at[low], 15)
    left(t_send.at[high], 16)

    arrived(first(g_in, 15), 6)
    g_sum = added(g_in, 16)
    g_zs[...] = g_sum
    g_z[z] = g_sum
    for d in RING:
        send(g_zs, g_z.at[z], 8, dev(core, at_z(d), me))
    arrived(first(h_in, 15), 5)
    h_sum = added(h_in, 16)
    h_zs[...] = h_sum
    h_z[z] = h_sum
    for d in RING:
        send(h_zs, h_z.at[z], 7, dev(core, at_z(d), me))
    left(first(g_in, 15), 6)
    left(first(h_in, 15), 5)

    arrived(t_z, 3)
    t_full[mine_t] = (t_send[...] + t_z[...]) * 0.25
    send(t_full.at[mine_t], t_full.at[mine_t], 9, twin)
    left(t_send, 3)
    for i in range(8, 11):
        loads[i].wait()

    arrived(l_full.at[other], 4)
    left(l_full.at[core], 4)
    arrived(first(g_z, 15), 8)
    slot = core * 16 + me
    g_full[slot] = added(g_z, 16)
    for dx, dy in PLANE:
        for c in (core, other):
            send(g_full.at[slot], g_full.at[slot], 10, dev(c, z, plane(dx, dy)))
    send(g_full.at[slot], g_full.at[slot], 10, twin)
    left(first(g_z, 15), 8)

    arrived(first(h_z, 15), 7)
    h_full[slot] = added(h_z, 16)
    for dx, dy in PLANE:
        for c in (core, other):
            send(h_full.at[slot], h_full.at[slot], 11, dev(c, z, plane(dx, dy)))
    send(h_full.at[slot], h_full.at[slot], 11, twin)
    left(first(h_z, 15), 7)

    arrived(t_full.at[other_t], 9)
    left(t_full.at[mine_t], 9)
    for i in range(2):
        for k in range(2):
            half = slice(512 * k, 512 * k + 512)
            o_squ[i, :, half], o_sqv[i, :, half] = nesterov(vsqw[i, :, half], t_full[2 * i + k], vsqm[i, :, half])
        for k in range(4):
            half = slice(512 * k, 512 * k + 512)
            o_bru[i, :, half], o_brv[i, :, half] = nesterov(vbrw[i, :, half], t_full[4 + 4 * i + k], vbrm[i, :, half])

    arrived(first(g_full, 31), 10)
    lanes = lax.broadcasted_iota(jnp.int32, (8, 128), 1)
    rows = lax.broadcasted_iota(jnp.int32, (8, 128), 0)
    blocks = [None] * 8
    for c in range(2):
        for half in range(2):
            tile = jnp.concatenate([g_full[16 * c + 8 * half + i] for i in range(8)], axis=0)
            blocks[4 * c + half] = pltpu.roll(tile, 64, 1)
            blocks[4 * c + 2 + half] = tile
    for b in range(8):
        blocks[b] = jnp.where(lanes >= 64, blocks[b], jnp.where(lanes == rows + 8 * b, 1.0, 0.0))
    inverse = jnp.concatenate(lower_inverse(blocks), axis=0)[:, :64]
    p_out[...] = dot(dot_t(jnp.concatenate([l_full[0], l_full[1]], axis=0).T, inverse), inverse)
    left(first(g_full, 31), 10)

    arrived(first(h_full, 31), 11)
    h_out[...] = h_full[...]
    left(first(h_full, 31), 11)


def communicate(*args):
    f32 = jnp.float32
    vmem = lambda *shape: pltpu.VMEM(shape, f32)
    dma = lambda n: pltpu.SemaphoreType.DMA((n,))
    shapes = [(2, 8, 1024)] * 2 + [(2, 8, 2048)] * 2 + [(128, 1024)] * 3 + [(128, 64), (32, 8, 256)]
    return pl.pallas_call(
        comm_kernel,
        name="exchange",
        out_shape=tuple(jax.ShapeDtypeStruct(s, f32) for s in shapes),
        in_specs=[pl.BlockSpec(memory_space=pltpu.HBM)] * 11,
        out_specs=tuple(pl.BlockSpec(memory_space=pltpu.VMEM) for _ in shapes),
        scratch_shapes=[
            vmem(2, 8, 1024), vmem(2, 8, 1024), vmem(2, 8, 2048), vmem(2, 8, 2048), vmem(2, 8, 1024), vmem(2, 8, 2048),
            vmem(128, 1024), vmem(128, 1024), vmem(64, 1024),
            vmem(128, 1024), vmem(2, 32, 128), vmem(2, 32, 128), vmem(2, 32, 128), vmem(2, 32, 128), vmem(2, 32, 128), vmem(2, 32, 128), vmem(2, 128, 128),
            vmem(12, 8, 512), vmem(6, 8, 512), vmem(6, 8, 512), vmem(2, 3, 8, 512), vmem(6, 8, 512), vmem(12, 8, 512),
            vmem(16, 8, 256), vmem(16, 8, 256), vmem(8, 256), vmem(16, 8, 256), vmem(32, 8, 256),
            vmem(16, 1, 128), vmem(16, 1, 128), vmem(1, 128), vmem(16, 1, 128), vmem(32, 1, 128),
            dma(11), dma(19), dma(19),
        ],
        compiler_params=pltpu.CompilerParams(collective_id=0, has_side_effects=True, vmem_limit_bytes=16 << 20),
    )(*(pltpu.with_memory_space_constraint(v, pltpu.HBM) for v in args))


def nesterov(weights, gradient, moment):
    velocity = momentum_decay * moment + gradient
    return (weights - outer_rate * (gradient + momentum_decay * velocity), velocity)


def update_kernel(squ, sqv, bru, brv, ew, em, corr, p, h, o_squ, o_sqv, o_bru, o_brv, o_eu, o_ev, o_er, eu, ev, er, sems):
    copies = [pltpu.make_async_copy(src, dst, sems.at[i]) for i, (src, dst) in enumerate(((squ, o_squ), (sqv, o_sqv), (bru, o_bru), (brv, o_brv)))]
    for copy in copies:
        copy.start()
    for cb in range(4):
        at = (slice(None), slice(256 * cb, 256 * cb + 256))
        step = dot(p[...], jnp.concatenate([h[16 * c + 4 * rb + cb] for c in range(2) for rb in range(4)], axis=0))
        eu[at], ev[at] = nesterov(ew[at], step, em[at])
        er[at] = corr[at] - step
        for i, (src, dst) in enumerate(((eu, o_eu), (ev, o_ev), (er, o_er))):
            copy = pltpu.make_async_copy(src.at[at], dst.at[at], sems.at[4 + 3 * cb + i])
            copy.start()
            copies.append(copy)
    for copy in copies:
        copy.wait()


def local(
    square_weights,
    square_copies,
    square_moment,
    broad_weights,
    broad_copies,
    broad_moment,
    embed_weights,
    embed_copies,
    embed_moment,
    embed_error,
    warm_start,
):
    ready = communicate(
        square_weights, square_copies[0], broad_weights, broad_copies[0], embed_weights, embed_copies[0], embed_error[0], warm_start,
        square_moment, broad_moment, embed_moment,
    )
    shapes = [square_weights.shape] * 2 + [broad_weights.shape] * 2 + [embed_weights.shape] * 3
    outs = pl.pallas_call(
        update_kernel,
        name="update",
        out_shape=tuple(jax.ShapeDtypeStruct(s, jnp.float32) for s in shapes),
        in_specs=[pl.BlockSpec(memory_space=pltpu.VMEM)] * 9,
        out_specs=tuple(pl.BlockSpec(memory_space=pltpu.HBM) for _ in shapes),
        scratch_shapes=[pltpu.VMEM((128, 1024), jnp.float32)] * 3 + [pltpu.SemaphoreType.DMA((16,))],
        compiler_params=pltpu.CompilerParams(vmem_limit_bytes=16 << 20),
    )(*ready)
    return (*outs[:6], outs[6][None])


def solution(mesh):
    in_specs = (
        P(None, "inner", None),
        P("replica", None, "inner", None),
        P(None, "inner", None),
        P(None, "inner", None),
        P("replica", None, "inner", None),
        P(None, "inner", None),
        P("inner", None),
        P("replica", "inner", None),
        P("inner", None),
        P("replica", "inner", None),
        P(),
    )
    out_specs = (
        P(None, "inner", None),
        P(None, "inner", None),
        P(None, "inner", None),
        P(None, "inner", None),
        P("inner", None),
        P("inner", None),
        P("replica", "inner", None),
    )
    return jax.shard_map(local, mesh=mesh, in_specs=in_specs, out_specs=out_specs, check_vma=False)
```

```python
import jax
import jax.numpy as jnp
from jax import lax
from jax.experimental import pallas as pl
from jax.experimental.pallas import tpu as pltpu
from jax.sharding import PartitionSpec as P

outer_rate = 0.7
momentum_decay = 0.9
MESH = pl.DeviceIdType.MESH
HIGHEST = lax.Precision.HIGHEST


def hops(dx, dy):
    return min(dx, 4 - dx) + min(dy, 4 - dy)


PLANE = sorted(((dx, dy) for dx in range(4) for dy in range(4) if dx or dy), key=lambda d: -hops(*d))
RING = sorted(range(1, 16), key=lambda d: -min(d, 16 - d))


def dot(a, b):
    return jnp.dot(a, b, precision=HIGHEST, preferred_element_type=jnp.float32)


def dot_t(a, b):
    return lax.dot_general(a, b, (((1,), (1,)), ((), ())), precision=HIGHEST, preferred_element_type=jnp.float32)


def sub(v, j):
    return jnp.broadcast_to(v[j : j + 1, :], v.shape)


def lower_inverse(a):
    rows = lax.broadcasted_iota(jnp.int32, (8, 128), 0)
    scale = []
    for kb in range(8):
        cols = {}
        for j in range(8):
            lane = 64 + 8 * kb + j
            for b in range(kb, 8):
                cols[b, j] = jnp.broadcast_to(a[b][:, lane : lane + 1], (8, 128))
        inv_pivots = jnp.ones((8, 128), jnp.float32)
        for j in range(8):
            inv = 1.0 / sub(cols[kb, j], j)
            inv_pivots = jnp.where(rows == j, inv, inv_pivots)
            row = sub(a[kb], j)
            later = [sub(cols[kb, i], j) for i in range(j + 1, 8)]
            for b in range(kb, 8):
                factor = cols[b, j] * inv
                if b == kb:
                    factor = jnp.where(rows > j, factor, 0.0)
                a[b] = a[b] - factor * row
                for i in range(j + 1, 8):
                    cols[b, i] = cols[b, i] - factor * later[i - j - 1]
        scale.append(jnp.sqrt(inv_pivots))
    return [a[b] * scale[b] for b in range(8)]


def comm_kernel(
    sqw, sqc, brw, brc, ew, ec, ee, ws, sqm, brm, em,
    o_squ, o_sqv, o_bru, o_brv, vew, vem, corr, p_out, h_out,
    vsqw, vsqc, vbrw, vbrc, vsqm, vbrm, vec, vee, vws,
    corr_in, l_part, l_twin, l_chip, l_in, l_relay, l_full, g_side, term, t_core, t_send, t_relay, t_z, t_full,
    h_part, h_in, h_zs, h_z, h_full, g_part, g_in, g_zs, g_z, g_full,
    load_sem, sent, got,
):
    rep, inn = lax.axis_index("replica"), lax.axis_index("inner")
    core, zhi = lax.rem(rep, 2), lax.div(rep, 2)
    zlo, x, y = lax.div(inn, 16), lax.rem(lax.div(inn, 4), 4), lax.rem(inn, 4)
    z, me = zhi * 8 + zlo, x * 4 + y
    other = 1 - core

    def plane(dx, dy):
        return lax.rem(x + dx, 4) * 4 + lax.rem(y + dy, 4)

    def at_z(d):
        return lax.rem(z + d, 16)

    def dev(c, zz, q):
        return (lax.div(zz, 8) * 2 + c, lax.rem(zz, 8) * 16 + q)

    twin, ahead, behind = dev(other, z, me), at_z(4), at_z(12)
    partners = [dev(other, ahead, me), dev(other, behind, me)] + [dev(core, at_z(d), me) for d in (4, 12, 3, 13, 2, 14, 1, 15)]
    for dx, dy in PLANE:
        partners += [dev(core, z, plane(dx, dy)), dev(other, z, plane(dx, dy))]
    partners.append(twin)
    loads = [
        pltpu.make_async_copy(src, dst, load_sem.at[i])
        for i, (src, dst) in enumerate((
            (ew, vew), (ec, vec), (ee, vee), (ws, vws), (sqw, vsqw), (sqc, vsqc), (brw, vbrw), (brc, vbrc), (sqm, vsqm), (brm, vbrm), (em, vem)
        ))
    ]
    for i in range(4):
        loads[i].start()
    barrier = pltpu.get_barrier_semaphore()
    for device in partners:
        pl.semaphore_signal(barrier, inc=1, device_id=device, device_id_type=MESH)
    for i in range(4, 11):
        loads[i].start()

    def send(src, dst, stage, device, arrival=None):
        pltpu.make_async_remote_copy(src, dst, sent.at[stage], got.at[stage] if arrival is None else arrival, device_id=device, device_id_type=MESH).start()

    def copies(ref, stage, arrival=None):
        return pltpu.make_async_remote_copy(ref, ref, sent.at[stage], got.at[stage] if arrival is None else arrival, device_id=twin, device_id_type=MESH)

    def arrived(ref, stage):
        copies(ref, stage).wait_recv()

    def left(ref, stage):
        copies(ref, stage).wait_send()

    def first(ref, n):
        return ref.at[pl.ds(0, n)]

    def added(ref, n):
        out = ref[0]
        for i in range(1, n):
            out = out + ref[i]
        return out

    for i in range(4):
        loads[i].wait()
    corr[...] = vew[...] - vec[...] + vee[...]
    part = dot_t(vws[...], corr[...])
    l_part[0] = part[:32]
    l_part[1] = part[32:]
    pl.semaphore_wait(barrier, len(partners))

    send(l_part.at[0], l_relay.at[0], 13, dev(core, ahead, me))
    send(l_part.at[1], l_relay.at[1], 14, dev(core, behind, me))
    send(l_part, l_twin, 17, twin)
    for i in range(4, 8):
        loads[i].wait()
    for i in range(2):
        for k in range(2):
            half = slice(512 * k, 512 * k + 512)
            term[2 * i + k] = vsqw[i, :, half] - vsqc[i, :, half]
        for k in range(4):
            half = slice(512 * k, 512 * k + 512)
            term[4 + 4 * i + k] = vbrw[i, :, half] - vbrc[i, :, half]
    mine_t, other_t = pl.ds(6 * core, 6), pl.ds(6 * other, 6)
    send(term.at[other_t], t_core, 1, twin)
    send(corr, corr_in, 2, twin)
    arrived(t_core, 1)
    t_send[...] = term[mine_t] + t_core[...]
    low, high, rest = pl.ds(0, 2), pl.ds(2, 2), pl.ds(4, 2)
    send(t_send.at[low], t_relay.at[0], 15, dev(core, ahead, me))
    send(t_send.at[high], t_relay.at[1], 16, dev(core, behind, me))
    arrived(l_relay.at[0], 13)
    send(l_relay.at[0], l_in.at[core], 0, dev(0, ahead, me))
    arrived(l_relay.at[1], 14)
    send(l_relay.at[1], l_in.at[core], 0, dev(1, behind, me))
    arrived(corr_in, 2)
    total = vec
    total[...] = corr[...] + corr_in[...]
    left(t_core, 1)
    left(corr, 2)
    arrived(l_twin, 17)
    left(l_part, 17)
    l_chip[...] = l_part[...] + l_twin[...]
    chip = jnp.concatenate([l_chip[0], l_chip[1]], axis=0) * 0.25
    nothing = jnp.zeros_like(chip)
    g_side[0] = jnp.concatenate([chip, nothing], axis=0)
    g_side[1] = jnp.concatenate([nothing, chip], axis=0)

    left(l_part.at[0], 13)
    left(l_part.at[1], 14)
    arrived(t_relay.at[0], 15)
    send(t_relay.at[0], t_z.at[low], 3, dev(core, ahead, me))
    arrived(t_relay.at[1], 16)
    send(t_relay.at[1], t_z.at[high], 3, dev(core, behind, me))
    left(t_send.at[low], 15)
    left(t_send.at[high], 16)
    arrived(l_in, 0)
    send(t_send.at[rest], t_z.at[rest], 18, dev(core, at_z(8), me), got.at[3])
    mine = (l_chip[core] + (l_in[0] + l_in[1])) * 0.25
    packed = dot_t(mine[:16], g_side[0]) + dot_t(mine[16:], g_side[1])
    for i in range(16):
        g_part[i] = packed[i : i + 1]
    for dx, dy in PLANE:
        q = plane(dx, dy)
        send(g_part.at[q], g_in.at[me], 6, dev(core, z, q))
    for cb in range(4):
        block = dot(mine, total[:, 256 * cb : 256 * cb + 256]) * 0.25
        for rb in range(4):
            h_part[4 * rb + cb] = block[8 * rb : 8 * rb + 8]
    for dx, dy in PLANE:
        q = plane(dx, dy)
        send(h_part.at[q], h_in.at[me], 5, dev(core, z, q))
    g_in[me] = g_part[me]
    h_in[me] = h_part[me]
    l_full[core] = mine
    send(l_full.at[core], l_full.at[core], 4, twin)
    left(l_in, 0)

    arrived(first(g_in, 15), 6)
    g_sum = added(g_in, 16)
    g_zs[...] = g_sum
    g_z[z] = g_sum
    for d in RING:
        send(g_zs, g_z.at[z], 8, dev(core, at_z(d), me))
    arrived(first(h_in, 15), 5)
    h_sum = added(h_in, 16)
    h_zs[...] = h_sum
    h_z[z] = h_sum
    for d in RING:
        send(h_zs, h_z.at[z], 7, dev(core, at_z(d), me))
    left(first(g_in, 15), 6)
    left(first(h_in, 15), 5)

    arrived(t_z, 3)
    t_full[mine_t] = (t_send[...] + t_z[...]) * 0.25
    send(t_full.at[mine_t], t_full.at[mine_t], 9, twin)
    left(t_send.at[pl.ds(0, 4)], 3)
    left(t_send.at[rest], 18)
    for i in range(8, 11):
        loads[i].wait()

    arrived(l_full.at[other], 4)
    left(l_full.at[core], 4)
    arrived(first(g_z, 15), 8)
    slot = core * 16 + me
    g_full[slot] = added(g_z, 16)
    for dx, dy in PLANE:
        for c in (core, other):
            send(g_full.at[slot], g_full.at[slot], 10, dev(c, z, plane(dx, dy)))
    send(g_full.at[slot], g_full.at[slot], 10, twin)
    left(first(g_z, 15), 8)

    arrived(first(h_z, 15), 7)
    h_full[slot] = added(h_z, 16)
    for c in (core, other):
        for dx, dy in PLANE:
            send(h_full.at[slot], h_full.at[slot], 11, dev(c, z, plane(dx, dy)))
    send(h_full.at[slot], h_full.at[slot], 11, twin)
    left(first(h_z, 15), 7)

    arrived(t_full.at[other_t], 9)
    left(t_full.at[mine_t], 9)
    for i in range(2):
        for k in range(2):
            half = slice(512 * k, 512 * k + 512)
            o_squ[i, :, half], o_sqv[i, :, half] = nesterov(vsqw[i, :, half], t_full[2 * i + k], vsqm[i, :, half])
        for k in range(4):
            half = slice(512 * k, 512 * k + 512)
            o_bru[i, :, half], o_brv[i, :, half] = nesterov(vbrw[i, :, half], t_full[4 + 4 * i + k], vbrm[i, :, half])

    arrived(first(g_full, 31), 10)
    lanes = lax.broadcasted_iota(jnp.int32, (8, 128), 1)
    rows = lax.broadcasted_iota(jnp.int32, (8, 128), 0)
    blocks = [None] * 8
    for c in range(2):
        for half in range(2):
            tile = jnp.concatenate([g_full[16 * c + 8 * half + i] for i in range(8)], axis=0)
            blocks[4 * c + half] = pltpu.roll(tile, 64, 1)
            blocks[4 * c + 2 + half] = tile
    for b in range(8):
        blocks[b] = jnp.where(lanes >= 64, blocks[b], jnp.where(lanes == rows + 8 * b, 1.0, 0.0))
    inverse = jnp.concatenate(lower_inverse(blocks), axis=0)[:, :64]
    p_out[...] = dot(dot_t(jnp.concatenate([l_full[0], l_full[1]], axis=0).T, inverse), inverse)
    left(first(g_full, 31), 10)

    arrived(first(h_full, 31), 11)
    h_out[...] = h_full[...]
    left(first(h_full, 31), 11)


def communicate(*args):
    f32 = jnp.float32
    vmem = lambda *shape: pltpu.VMEM(shape, f32)
    dma = lambda n: pltpu.SemaphoreType.DMA((n,))
    shapes = [(2, 8, 1024)] * 2 + [(2, 8, 2048)] * 2 + [(128, 1024)] * 3 + [(128, 64), (32, 8, 256)]
    return pl.pallas_call(
        comm_kernel,
        name="exchange",
        out_shape=tuple(jax.ShapeDtypeStruct(s, f32) for s in shapes),
        in_specs=[pl.BlockSpec(memory_space=pltpu.HBM)] * 11,
        out_specs=tuple(pl.BlockSpec(memory_space=pltpu.VMEM) for _ in shapes),
        scratch_shapes=[
            vmem(2, 8, 1024), vmem(2, 8, 1024), vmem(2, 8, 2048), vmem(2, 8, 2048), vmem(2, 8, 1024), vmem(2, 8, 2048),
            vmem(128, 1024), vmem(128, 1024), vmem(64, 1024),
            vmem(128, 1024), vmem(2, 32, 128), vmem(2, 32, 128), vmem(2, 32, 128), vmem(2, 32, 128), vmem(2, 32, 128), vmem(2, 32, 128), vmem(2, 128, 128),
            vmem(12, 8, 512), vmem(6, 8, 512), vmem(6, 8, 512), vmem(2, 2, 8, 512), vmem(6, 8, 512), vmem(12, 8, 512),
            vmem(16, 8, 256), vmem(16, 8, 256), vmem(8, 256), vmem(16, 8, 256), vmem(32, 8, 256),
            vmem(16, 1, 128), vmem(16, 1, 128), vmem(1, 128), vmem(16, 1, 128), vmem(32, 1, 128),
            dma(11), dma(19), dma(19),
        ],
        compiler_params=pltpu.CompilerParams(collective_id=0, has_side_effects=True, vmem_limit_bytes=16 << 20),
    )(*(pltpu.with_memory_space_constraint(v, pltpu.HBM) for v in args))


def nesterov(weights, gradient, moment):
    velocity = momentum_decay * moment + gradient
    return (weights - outer_rate * (gradient + momentum_decay * velocity), velocity)


def update_kernel(squ, sqv, bru, brv, ew, em, corr, p, h, o_squ, o_sqv, o_bru, o_brv, o_eu, o_ev, o_er, eu, ev, er, sems):
    copies = [pltpu.make_async_copy(src, dst, sems.at[i]) for i, (src, dst) in enumerate(((squ, o_squ), (sqv, o_sqv), (bru, o_bru), (brv, o_brv)))]
    for copy in copies:
        copy.start()
    for cb in range(4):
        at = (slice(None), slice(256 * cb, 256 * cb + 256))
        step = dot(p[...], jnp.concatenate([h[16 * c + 4 * rb + cb] for c in range(2) for rb in range(4)], axis=0))
        eu[at], ev[at] = nesterov(ew[at], step, em[at])
        er[at] = corr[at] - step
        for i, (src, dst) in enumerate(((eu, o_eu), (ev, o_ev), (er, o_er))):
            copy = pltpu.make_async_copy(src.at[at], dst.at[at], sems.at[4 + 3 * cb + i])
            copy.start()
            copies.append(copy)
    for copy in copies:
        copy.wait()


def local(
    square_weights,
    square_copies,
    square_moment,
    broad_weights,
    broad_copies,
    broad_moment,
    embed_weights,
    embed_copies,
    embed_moment,
    embed_error,
    warm_start,
):
    ready = communicate(
        square_weights, square_copies[0], broad_weights, broad_copies[0], embed_weights, embed_copies[0], embed_error[0], warm_start,
        square_moment, broad_moment, embed_moment,
    )
    shapes = [square_weights.shape] * 2 + [broad_weights.shape] * 2 + [embed_weights.shape] * 3
    outs = pl.pallas_call(
        update_kernel,
        name="update",
        out_shape=tuple(jax.ShapeDtypeStruct(s, jnp.float32) for s in shapes),
        in_specs=[pl.BlockSpec(memory_space=pltpu.VMEM)] * 9,
        out_specs=tuple(pl.BlockSpec(memory_space=pltpu.HBM) for _ in shapes),
        scratch_shapes=[pltpu.VMEM((128, 1024), jnp.float32)] * 3 + [pltpu.SemaphoreType.DMA((16,))],
        compiler_params=pltpu.CompilerParams(vmem_limit_bytes=16 << 20),
    )(*ready)
    return (*outs[:6], outs[6][None])


def solution(mesh):
    in_specs = (
        P(None, "inner", None),
        P("replica", None, "inner", None),
        P(None, "inner", None),
        P(None, "inner", None),
        P("replica", None, "inner", None),
        P(None, "inner", None),
        P("inner", None),
        P("replica", "inner", None),
        P("inner", None),
        P("replica", "inner", None),
        P(),
    )
    out_specs = (
        P(None, "inner", None),
        P(None, "inner", None),
        P(None, "inner", None),
        P(None, "inner", None),
        P("inner", None),
        P("inner", None),
        P("replica", "inner", None),
    )
    return jax.shard_map(local, mesh=mesh, in_specs=in_specs, out_specs=out_specs, check_vma=False)
```

```python
import jax
import jax.numpy as jnp
from jax import lax
from jax.experimental import pallas as pl
from jax.experimental.pallas import tpu as pltpu
from jax.sharding import PartitionSpec as P

outer_rate = 0.7
momentum_decay = 0.9
MESH = pl.DeviceIdType.MESH
HIGHEST = lax.Precision.HIGHEST


def hops(dx, dy):
    return min(dx, 4 - dx) + min(dy, 4 - dy)


PLANE = sorted(((dx, dy) for dx in range(4) for dy in range(4) if dx or dy), key=lambda d: -hops(*d))
RING = sorted(range(1, 16), key=lambda d: -min(d, 16 - d))


def dot(a, b):
    return jnp.dot(a, b, precision=HIGHEST, preferred_element_type=jnp.float32)


def dot_t(a, b):
    return lax.dot_general(a, b, (((1,), (1,)), ((), ())), precision=HIGHEST, preferred_element_type=jnp.float32)


def sub(v, j):
    return jnp.broadcast_to(v[j : j + 1, :], v.shape)


def lower_inverse(a):
    rows = lax.broadcasted_iota(jnp.int32, (8, 128), 0)
    scale = []
    for kb in range(8):
        cols = {}
        for j in range(8):
            lane = 64 + 8 * kb + j
            for b in range(kb, 8):
                cols[b, j] = jnp.broadcast_to(a[b][:, lane : lane + 1], (8, 128))
        inv_pivots = jnp.ones((8, 128), jnp.float32)
        for j in range(8):
            inv = 1.0 / sub(cols[kb, j], j)
            inv_pivots = jnp.where(rows == j, inv, inv_pivots)
            row = sub(a[kb], j)
            later = [sub(cols[kb, i], j) for i in range(j + 1, 8)]
            for b in range(kb, 8):
                factor = cols[b, j] * inv
                if b == kb:
                    factor = jnp.where(rows > j, factor, 0.0)
                a[b] = a[b] - factor * row
                for i in range(j + 1, 8):
                    cols[b, i] = cols[b, i] - factor * later[i - j - 1]
        scale.append(jnp.sqrt(inv_pivots))
    return [a[b] * scale[b] for b in range(8)]


def comm_kernel(
    sqw, sqc, brw, brc, ew, ec, ee, ws, sqm, brm, em,
    o_squ, o_sqv, o_bru, o_brv, vew, vem, corr, p_out, h_out,
    vsqw, vsqc, vbrw, vbrc, vsqm, vbrm, vec, vee, vws,
    corr_in, l_part, l_twin, l_chip, l_in, l_relay, l_full, g_side, term, t_core, t_send, t_relay, t_z, t_full,
    h_part, h_in, h_zs, h_z, h_full, g_part, g_in, g_zs, g_z, g_full,
    load_sem, sent, got,
):
    rep, inn = lax.axis_index("replica"), lax.axis_index("inner")
    core, zhi = lax.rem(rep, 2), lax.div(rep, 2)
    zlo, x, y = lax.div(inn, 16), lax.rem(lax.div(inn, 4), 4), lax.rem(inn, 4)
    z, me = zhi * 8 + zlo, x * 4 + y
    other = 1 - core

    def plane(dx, dy):
        return lax.rem(x + dx, 4) * 4 + lax.rem(y + dy, 4)

    def at_z(d):
        return lax.rem(z + d, 16)

    def dev(c, zz, q):
        return (lax.div(zz, 8) * 2 + c, lax.rem(zz, 8) * 16 + q)

    twin, ahead, behind = dev(other, z, me), at_z(4), at_z(12)
    partners = [dev(other, ahead, me), dev(other, behind, me)] + [dev(core, at_z(d), me) for d in (4, 12, 3, 13, 2, 14, 1, 15)]
    for dx, dy in PLANE:
        partners += [dev(core, z, plane(dx, dy)), dev(other, z, plane(dx, dy))]
    partners.append(twin)
    loads = [
        pltpu.make_async_copy(src, dst, load_sem.at[i])
        for i, (src, dst) in enumerate((
            (ew, vew), (ec, vec), (ee, vee), (ws, vws), (sqw, vsqw), (sqc, vsqc), (brw, vbrw), (brc, vbrc), (sqm, vsqm), (brm, vbrm), (em, vem)
        ))
    ]
    for i in range(4):
        loads[i].start()
    barrier = pltpu.get_barrier_semaphore()
    for device in partners:
        pl.semaphore_signal(barrier, inc=1, device_id=device, device_id_type=MESH)
    for i in range(4, 11):
        loads[i].start()

    def send(src, dst, stage, device, arrival=None):
        pltpu.make_async_remote_copy(src, dst, sent.at[stage], got.at[stage] if arrival is None else arrival, device_id=device, device_id_type=MESH).start()

    def copies(ref, stage, arrival=None):
        return pltpu.make_async_remote_copy(ref, ref, sent.at[stage], got.at[stage] if arrival is None else arrival, device_id=twin, device_id_type=MESH)

    def arrived(ref, stage):
        copies(ref, stage).wait_recv()

    def left(ref, stage):
        copies(ref, stage).wait_send()

    def first(ref, n):
        return ref.at[pl.ds(0, n)]

    def added(ref, n):
        out = ref[0]
        for i in range(1, n):
            out = out + ref[i]
        return out

    for i in range(4):
        loads[i].wait()
    corr[...] = vew[...] - vec[...] + vee[...]
    part = dot_t(vws[...], corr[...])
    l_part[0] = part[:32]
    l_part[1] = part[32:]
    pl.semaphore_wait(barrier, len(partners))

    send(l_part.at[0], l_relay.at[0], 13, dev(core, ahead, me))
    send(l_part.at[1], l_relay.at[1], 14, dev(core, behind, me))
    send(l_part, l_twin, 17, twin)
    for i in range(4, 8):
        loads[i].wait()
    for i in range(2):
        for k in range(2):
            half = slice(512 * k, 512 * k + 512)
            term[2 * i + k] = vsqw[i, :, half] - vsqc[i, :, half]
        for k in range(4):
            half = slice(512 * k, 512 * k + 512)
            term[4 + 4 * i + k] = vbrw[i, :, half] - vbrc[i, :, half]
    mine_t, other_t = pl.ds(6 * core, 6), pl.ds(6 * other, 6)
    send(term.at[other_t], t_core, 1, twin)
    send(corr, corr_in, 2, twin)
    arrived(t_core, 1)
    t_send[...] = term[mine_t] + t_core[...]
    low, high, rest = pl.ds(0, 2), pl.ds(2, 2), pl.ds(4, 2)
    send(t_send.at[low], t_relay.at[0], 15, dev(core, ahead, me))
    send(t_send.at[high], t_relay.at[1], 16, dev(core, behind, me))
    middle = jnp.logical_and(z >= 4, z < 12)

    def pass_left(way):
        arrived(l_relay.at[way], 13 + way)
        send(l_relay.at[way], l_in.at[core], 0, dev(way, (ahead, behind)[way], me))

    def pass_term(way):
        arrived(t_relay.at[way], 15 + way)
        send(t_relay.at[way], t_z.at[(low, high)[way]], 3, dev(core, (ahead, behind)[way], me))

    def earlier_first(step):
        @pl.when(middle)
        def _():
            step(0)
            step(1)

        @pl.when(jnp.logical_not(middle))
        def _():
            step(1)
            step(0)

    earlier_first(pass_left)
    arrived(corr_in, 2)
    total = vec
    total[...] = corr[...] + corr_in[...]
    left(t_core, 1)
    left(corr, 2)
    arrived(l_twin, 17)
    left(l_part, 17)
    l_chip[...] = l_part[...] + l_twin[...]
    chip = jnp.concatenate([l_chip[0], l_chip[1]], axis=0) * 0.25
    nothing = jnp.zeros_like(chip)
    g_side[0] = jnp.concatenate([chip, nothing], axis=0)
    g_side[1] = jnp.concatenate([nothing, chip], axis=0)

    left(l_part.at[0], 13)
    left(l_part.at[1], 14)
    earlier_first(pass_term)
    left(t_send.at[low], 15)
    left(t_send.at[high], 16)
    arrived(l_in, 0)
    send(t_send.at[rest], t_z.at[rest], 18, dev(core, at_z(8), me), got.at[3])
    mine = (l_chip[core] + (l_in[0] + l_in[1])) * 0.25
    packed = dot_t(mine[:16], g_side[0]) + dot_t(mine[16:], g_side[1])
    for i in range(16):
        g_part[i] = packed[i : i + 1]
    for dx, dy in PLANE:
        q = plane(dx, dy)
        send(g_part.at[q], g_in.at[me], 6, dev(core, z, q))
    for cb in range(4):
        block = dot(mine, total[:, 256 * cb : 256 * cb + 256]) * 0.25
        for rb in range(4):
            h_part[4 * rb + cb] = block[8 * rb : 8 * rb + 8]
    for dx, dy in PLANE:
        q = plane(dx, dy)
        send(h_part.at[q], h_in.at[me], 5, dev(core, z, q))
    g_in[me] = g_part[me]
    h_in[me] = h_part[me]
    l_full[core] = mine
    send(l_full.at[core], l_full.at[core], 4, twin)
    left(l_in, 0)

    arrived(first(g_in, 15), 6)
    g_sum = added(g_in, 16)
    g_zs[...] = g_sum
    g_z[z] = g_sum
    for d in RING:
        send(g_zs, g_z.at[z], 8, dev(core, at_z(d), me))
    arrived(first(h_in, 15), 5)
    h_sum = added(h_in, 16)
    h_zs[...] = h_sum
    h_z[z] = h_sum
    for d in RING:
        send(h_zs, h_z.at[z], 7, dev(core, at_z(d), me))
    left(first(g_in, 15), 6)
    left(first(h_in, 15), 5)

    arrived(t_z, 3)
    t_full[mine_t] = (t_send[...] + t_z[...]) * 0.25
    send(t_full.at[mine_t], t_full.at[mine_t], 9, twin)
    left(t_send.at[pl.ds(0, 4)], 3)
    left(t_send.at[rest], 18)
    for i in range(8, 11):
        loads[i].wait()

    arrived(l_full.at[other], 4)
    left(l_full.at[core], 4)
    arrived(first(g_z, 15), 8)
    slot = core * 16 + me
    g_full[slot] = added(g_z, 16)
    for dx, dy in PLANE:
        for c in (core, other):
            send(g_full.at[slot], g_full.at[slot], 10, dev(c, z, plane(dx, dy)))
    send(g_full.at[slot], g_full.at[slot], 10, twin)
    left(first(g_z, 15), 8)

    arrived(first(h_z, 15), 7)
    h_full[slot] = added(h_z, 16)
    for c in (core, other):
        for dx, dy in PLANE:
            send(h_full.at[slot], h_full.at[slot], 11, dev(c, z, plane(dx, dy)))
    send(h_full.at[slot], h_full.at[slot], 11, twin)
    left(first(h_z, 15), 7)

    arrived(t_full.at[other_t], 9)
    left(t_full.at[mine_t], 9)
    for i in range(2):
        for k in range(2):
            half = slice(512 * k, 512 * k + 512)
            o_squ[i, :, half], o_sqv[i, :, half] = nesterov(vsqw[i, :, half], t_full[2 * i + k], vsqm[i, :, half])
        for k in range(4):
            half = slice(512 * k, 512 * k + 512)
            o_bru[i, :, half], o_brv[i, :, half] = nesterov(vbrw[i, :, half], t_full[4 + 4 * i + k], vbrm[i, :, half])

    arrived(first(g_full, 31), 10)
    lanes = lax.broadcasted_iota(jnp.int32, (8, 128), 1)
    rows = lax.broadcasted_iota(jnp.int32, (8, 128), 0)
    blocks = [None] * 8
    for c in range(2):
        for half in range(2):
            tile = jnp.concatenate([g_full[16 * c + 8 * half + i] for i in range(8)], axis=0)
            blocks[4 * c + half] = pltpu.roll(tile, 64, 1)
            blocks[4 * c + 2 + half] = tile
    for b in range(8):
        blocks[b] = jnp.where(lanes >= 64, blocks[b], jnp.where(lanes == rows + 8 * b, 1.0, 0.0))
    inverse = jnp.concatenate(lower_inverse(blocks), axis=0)[:, :64]
    p_out[...] = dot(dot_t(jnp.concatenate([l_full[0], l_full[1]], axis=0).T, inverse), inverse)
    left(first(g_full, 31), 10)

    arrived(first(h_full, 31), 11)
    h_out[...] = h_full[...]
    left(first(h_full, 31), 11)


def communicate(*args):
    f32 = jnp.float32
    vmem = lambda *shape: pltpu.VMEM(shape, f32)
    dma = lambda n: pltpu.SemaphoreType.DMA((n,))
    shapes = [(2, 8, 1024)] * 2 + [(2, 8, 2048)] * 2 + [(128, 1024)] * 3 + [(128, 64), (32, 8, 256)]
    return pl.pallas_call(
        comm_kernel,
        name="exchange",
        out_shape=tuple(jax.ShapeDtypeStruct(s, f32) for s in shapes),
        in_specs=[pl.BlockSpec(memory_space=pltpu.HBM)] * 11,
        out_specs=tuple(pl.BlockSpec(memory_space=pltpu.VMEM) for _ in shapes),
        scratch_shapes=[
            vmem(2, 8, 1024), vmem(2, 8, 1024), vmem(2, 8, 2048), vmem(2, 8, 2048), vmem(2, 8, 1024), vmem(2, 8, 2048),
            vmem(128, 1024), vmem(128, 1024), vmem(64, 1024),
            vmem(128, 1024), vmem(2, 32, 128), vmem(2, 32, 128), vmem(2, 32, 128), vmem(2, 32, 128), vmem(2, 32, 128), vmem(2, 32, 128), vmem(2, 128, 128),
            vmem(12, 8, 512), vmem(6, 8, 512), vmem(6, 8, 512), vmem(2, 2, 8, 512), vmem(6, 8, 512), vmem(12, 8, 512),
            vmem(16, 8, 256), vmem(16, 8, 256), vmem(8, 256), vmem(16, 8, 256), vmem(32, 8, 256),
            vmem(16, 1, 128), vmem(16, 1, 128), vmem(1, 128), vmem(16, 1, 128), vmem(32, 1, 128),
            dma(11), dma(19), dma(19),
        ],
        compiler_params=pltpu.CompilerParams(collective_id=0, has_side_effects=True, vmem_limit_bytes=16 << 20),
    )(*(pltpu.with_memory_space_constraint(v, pltpu.HBM) for v in args))


def nesterov(weights, gradient, moment):
    velocity = momentum_decay * moment + gradient
    return (weights - outer_rate * (gradient + momentum_decay * velocity), velocity)


def update_kernel(squ, sqv, bru, brv, ew, em, corr, p, h, o_squ, o_sqv, o_bru, o_brv, o_eu, o_ev, o_er, eu, ev, er, sems):
    copies = [pltpu.make_async_copy(src, dst, sems.at[i]) for i, (src, dst) in enumerate(((squ, o_squ), (sqv, o_sqv), (bru, o_bru), (brv, o_brv)))]
    for copy in copies:
        copy.start()
    for cb in range(4):
        at = (slice(None), slice(256 * cb, 256 * cb + 256))
        step = dot(p[...], jnp.concatenate([h[16 * c + 4 * rb + cb] for c in range(2) for rb in range(4)], axis=0))
        eu[at], ev[at] = nesterov(ew[at], step, em[at])
        er[at] = corr[at] - step
        for i, (src, dst) in enumerate(((eu, o_eu), (ev, o_ev), (er, o_er))):
            copy = pltpu.make_async_copy(src.at[at], dst.at[at], sems.at[4 + 3 * cb + i])
            copy.start()
            copies.append(copy)
    for copy in copies:
        copy.wait()


def local(
    square_weights,
    square_copies,
    square_moment,
    broad_weights,
    broad_copies,
    broad_moment,
    embed_weights,
    embed_copies,
    embed_moment,
    embed_error,
    warm_start,
):
    ready = communicate(
        square_weights, square_copies[0], broad_weights, broad_copies[0], embed_weights, embed_copies[0], embed_error[0], warm_start,
        square_moment, broad_moment, embed_moment,
    )
    shapes = [square_weights.shape] * 2 + [broad_weights.shape] * 2 + [embed_weights.shape] * 3
    outs = pl.pallas_call(
        update_kernel,
        name="update",
        out_shape=tuple(jax.ShapeDtypeStruct(s, jnp.float32) for s in shapes),
        in_specs=[pl.BlockSpec(memory_space=pltpu.VMEM)] * 9,
        out_specs=tuple(pl.BlockSpec(memory_space=pltpu.HBM) for _ in shapes),
        scratch_shapes=[pltpu.VMEM((128, 1024), jnp.float32)] * 3 + [pltpu.SemaphoreType.DMA((16,))],
        compiler_params=pltpu.CompilerParams(vmem_limit_bytes=16 << 20),
    )(*ready)
    return (*outs[:6], outs[6][None])


def solution(mesh):
    in_specs = (
        P(None, "inner", None),
        P("replica", None, "inner", None),
        P(None, "inner", None),
        P(None, "inner", None),
        P("replica", None, "inner", None),
        P(None, "inner", None),
        P("inner", None),
        P("replica", "inner", None),
        P("inner", None),
        P("replica", "inner", None),
        P(),
    )
    out_specs = (
        P(None, "inner", None),
        P(None, "inner", None),
        P(None, "inner", None),
        P(None, "inner", None),
        P("inner", None),
        P("inner", None),
        P("replica", "inner", None),
    )
    return jax.shard_map(local, mesh=mesh, in_specs=in_specs, out_specs=out_specs, check_vma=False)
```
